32 devices in a mesh: parts: 2 (over x), elec: 4 (over y, core), walk: 4 (over z).
Axes of the slice: x: 2, y: 2, z: 4, core: 2. Of those that a mesh axis runs over, the one named last changes fastest.
Arguments:
- elec_pos: float32 [3, 32, 512], P(None, ('parts', 'walk'), 'elec'), parts along dimension 1, may hold values from -8 to 8
- atom_pos: float32 [200, 3], P(('parts', 'elec')), parts along dimension 0, may hold values from -8 to 8
- atom_emb: float32 [200, 256], P(('parts', 'elec')), parts along dimension 0, may hold values from -6 to 6
- spin_emb: float32 [2, 256], replicated, may hold values from -6 to 6
- spin: int32 [1024], P(('parts', 'elec')), parts along dimension 0, may hold values from 0 to 1, as said below
- near_atoms: int32 [16, 2], P('parts'), parts along dimension 0, may hold values from 0 to 3
- pair_list: int32 [16, 4], P('parts'), parts along dimension 0, may hold values from 0 to 7, as said below
- pair_count: int32 [16], P('parts'), parts along dimension 0, may hold values from 1 to 4, as said below
- w_query: bfloat16 [256, 256], replicated, may hold values from -64 to 64
- w_key: bfloat16 [256, 256], replicated, may hold values from -0.375 to 0.375
- w_value: bfloat16 [256, 256], replicated, may hold values from -0.375 to 0.375
- w_out: bfloat16 [256, 256], replicated, may hold values from -0.375 to 0.375
- w_orb: bfloat16 [2, 256, 1024], replicated, may hold values from -0.375 to 0.375
- target: bfloat16 [32, 512, 1024], P(('parts', 'walk'), 'elec'), parts along dimension 0, may hold values from -6 to 6
Outputs:
- grad_orb: float32 [4, 256, 1024], P('parts'), parts along dimension 0
- grad_out: float32 [512, 256], P('parts'), parts along dimension 0
- loss: float32 [2], P('parts'), parts along dimension 0
The draws below stay inside these ranges and needn't reach their ends.
There are 2 independent parts, one for each index of `parts`. The reference program is written for one: setup_inputs(seed, part) draws one part's arguments, and reference() takes and returns one part's arrays. A program takes and returns all parts, laid end to end along the dimension named above; an argument that names none is the same for every part. Nothing has to cross between parts.
Inputs may be any that keep to these rules, and one draw needn't show every extreme that they name: `pair_list`: row b lists 4 distinct blocks, the first being b itself; every listed c has c // 2 equal to b // 2 or one more or one less than it, modulo 8 / 2. Only the first pair_count[b] entries of row b are listed; some block lists all 4. Each aligned run of 128 electrons holds exactly half of each spin.
All inputs are finite; a program needn't handle non-finite values.
Results may differ from the reference program's by a relative error of at most 0.002.
Values may be sent and summed in bfloat16 or wider, within the bound.
A program may use at most 64 MiB of HBM per device.

```python
import math
import jax
import jax.numpy as jnp
from jax import lax

D = 256
HEADS = 16
KORB = 1024
BLOCK = 64
BPD = 2
ATOM_DEV = 25
NEAR = 2
KMAX = 4
NBLK = 8
NE = 512
ATOMS = 100
WALKERS = 16


def pair_tables(key):
    blocks = jnp.arange(NBLK)
    group_total = NBLK // BPD
    home_device = blocks // BPD
    offsets = jnp.array([-1, 0, 1], jnp.int32)
    candidates = ((home_device[:, None, None] + offsets[None, :, None]) % group_total * BPD + jnp.arange(BPD)[None, None, :]).reshape(NBLK, 3 * BPD)
    row_keys = jax.random.split(jax.random.fold_in(key, 11), NBLK)
    priority = jax.vmap(lambda row_key: jax.random.permutation(row_key, 3 * BPD))(row_keys)
    priority = jnp.where(candidates == blocks[:, None], -1, priority)
    ranked = jnp.argsort(priority, axis=1, stable=True)
    chosen = jnp.take_along_axis(candidates, ranked, axis=1)[:, :KMAX]
    counts = jax.random.randint(jax.random.fold_in(key, 12), (NBLK,), 1, KMAX + 1)
    full_block = jax.random.randint(jax.random.fold_in(key, 13), (), 0, NBLK)
    counts = jnp.where(blocks == full_block, KMAX, counts)
    return (chosen.astype(jnp.int32), counts.astype(jnp.int32))


def draw_pair_list(key, part):
    return pair_tables(key)[0]


def draw_pair_count(key, part):
    return pair_tables(key)[1]


def draw_spin(key, part):
    run_rows = BPD * BLOCK
    run_count = NE // run_rows
    run_keys = jax.random.split(jax.random.fold_in(key, 21), run_count)
    orders = jax.vmap(lambda run_key: jax.random.permutation(run_key, run_rows))(run_keys)
    return (orders >= run_rows // 2).astype(jnp.int32).reshape(NE)


def draw_w_query(key, part):
    entries = jax.random.truncated_normal(key, -4.0, 4.0, (D, D), jnp.float32) / math.sqrt(D)
    return entries.astype(jnp.bfloat16)


def with_ends(values, rng, smallest, high):
    spot = [jax.random.randint(jax.random.fold_in(rng, axis), (), 0, length) for axis, length in enumerate(values.shape)]
    widest = values.shape.index(max(values.shape))
    neighbour = spot[:widest] + [(spot[widest] + 1) % values.shape[widest]] + spot[widest + 1:]
    return values.at[tuple(spot)].set(smallest).at[tuple(neighbour)].set(high)


def level_of(stream_key, shape, pieces, least, top_value):
    loudness, own = 1.0, jax.random.fold_in(stream_key, 6)
    for axis_at, blocks in pieces:
        heights = jnp.exp(jax.random.uniform(jax.random.fold_in(own, axis_at), (blocks,), jnp.float32, least / len(pieces), top_value / len(pieces)))
        loudness = loudness * jnp.repeat(heights, shape[axis_at] // blocks).reshape([-1 if axis == axis_at else 1 for axis in range(len(shape))])
    return loudness


def noise(stream_key, dims, deviation, limit, shards=(), dtype=jnp.bfloat16):
    values = deviation * jax.random.normal(stream_key, dims, jnp.float32)
    if shards:
        values = values * level_of(stream_key, dims, shards, -0.22, 0.18)
    return jnp.clip(values, -limit, limit).astype(dtype)


def setup_inputs(seed: int = 0, part: int = 0) -> dict:
    streams_of = jax.random.split(jax.random.key(seed), 15)
    part_keys = jax.random.split(jax.random.fold_in(streams_of[14], part), 15)
    elec_pos = noise(part_keys[0], (3, WALKERS, NE), 1.5, 8.0, ((1, 4), (2, 4)), jnp.float32)
    atom_pos = noise(part_keys[1], (ATOMS, 3), 1.5, 8.0, ((0, 4),), jnp.float32)
    atom_emb = noise(part_keys[2], (ATOMS, D), 1.0, 6.0, ((0, 4),), jnp.float32)
    spin_emb = noise(streams_of[3], (2, D), 1.0, 6.0, (), jnp.float32)
    spin = draw_spin(jax.random.fold_in(jax.random.fold_in(streams_of[14], part), 71), part)
    near_atoms = with_ends(jax.random.randint(part_keys[5], (NBLK, NEAR), 0, NBLK // BPD), jax.random.fold_in(part_keys[5], 1), 0, (NBLK // BPD) - 1).astype(jnp.int32)
    pair_list = draw_pair_list(jax.random.fold_in(jax.random.fold_in(streams_of[14], part), 71), part)
    pair_count = draw_pair_count(jax.random.fold_in(jax.random.fold_in(streams_of[14], part), 71), part)
    w_query = draw_w_query(jax.random.fold_in(streams_of[14], 71), part)
    w_key = noise(streams_of[9], (D, D), D ** -0.5, 0.375)
    w_value = noise(streams_of[10], (D, D), D ** -0.5, 0.375)
    w_out = noise(streams_of[11], (D, D), D ** -0.5, 0.375)
    w_orb = noise(streams_of[12], (2, D, KORB), D ** -0.5, 0.375)
    target = noise(part_keys[13], (WALKERS, NE, KORB), 1.0, 6.0, ((0, 4), (1, 4)))
    return {"elec_pos": elec_pos, "atom_pos": atom_pos, "atom_emb": atom_emb, "spin_emb": spin_emb, "spin": spin, "near_atoms": near_atoms, "pair_list": pair_list, "pair_count": pair_count, "w_query": w_query, "w_key": w_key, "w_value": w_value, "w_out": w_out, "w_orb": w_orb, "target": target}


def atom_states(elec_pos, atom_pos, atom_emb, near_atoms):
    block_count = near_atoms.shape[0]
    walkers = elec_pos.shape[1]
    group_count = atom_pos.shape[0] // ATOM_DEV
    near_pos = jnp.take(atom_pos.reshape(group_count, ATOM_DEV, 3), near_atoms, axis=0).reshape(block_count, NEAR * ATOM_DEV, 3)
    near_emb = jnp.take(atom_emb.reshape(group_count, ATOM_DEV, atom_emb.shape[1]), near_atoms, axis=0).reshape(block_count, NEAR * ATOM_DEV, atom_emb.shape[1])
    positions = elec_pos.reshape(3, walkers, block_count, BLOCK)
    distance = jnp.zeros((walkers, block_count, BLOCK, NEAR * ATOM_DEV), jnp.float32)
    for axis_id in range(3):
        spacing = positions[axis_id][..., None] - near_pos[None, :, None, :, axis_id]
        distance = distance + spacing * spacing
    closeness = 1.0 / (1.0 + distance)
    return jnp.einsum('wbea,bad->wbed', closeness, near_emb, precision=lax.Precision.HIGHEST)

def reference(elec_pos, atom_pos, atom_emb, spin_emb, spin, near_atoms, pair_list, pair_count, w_query, w_key, w_value, w_out, w_orb, target):
    walkers = elec_pos.shape[1]
    electrons = elec_pos.shape[2]
    model_width = w_query.shape[0]
    head_size = model_width // HEADS
    row_total = walkers * electrons
    atom_term = atom_states(elec_pos, atom_pos, atom_emb, near_atoms).reshape(walkers, electrons, model_width)
    spin_rows = jnp.where(spin[:, None] == 1, spin_emb[1][None, :], spin_emb[0][None, :])
    hidden = (atom_term + spin_rows[None]).astype(jnp.bfloat16)
    flat_rows = hidden.reshape(row_total, model_width)
    queries = jnp.dot(flat_rows, w_query, preferred_element_type=jnp.float32).astype(jnp.bfloat16).reshape(walkers, electrons, HEADS, head_size)
    key_rows = jnp.dot(flat_rows, w_key, preferred_element_type=jnp.float32).astype(jnp.bfloat16).reshape(walkers, electrons, HEADS, head_size)
    value_rows = jnp.dot(flat_rows, w_value, preferred_element_type=jnp.float32).astype(jnp.bfloat16).reshape(walkers, electrons, HEADS, head_size)
    block_count = pair_list.shape[0]
    slot_ids = jnp.arange(KMAX)
    in_list = slot_ids[None, :] < pair_count[:, None]
    listed = jnp.any((pair_list[:, :, None] == jnp.arange(block_count)[None, None, :]) & in_list[:, :, None], axis=1)
    allowed = jnp.repeat(jnp.repeat(listed, BLOCK, axis=0), BLOCK, axis=1)
    score_scale = 1.0 / math.sqrt(head_size)

    def attend(operands):
        query_one, key_one, value_one = operands
        scores = jnp.einsum('qhd,khd->qhk', query_one.astype(jnp.float32), key_one.astype(jnp.float32)) * score_scale
        key_mask = allowed[:, None, :]
        scores = jnp.where(key_mask, scores, -1e+30)
        row_max = lax.optimization_barrier(jnp.max(scores, axis=2, keepdims=True))
        weights = jnp.where(key_mask, jnp.exp(scores - row_max), 0.0)
        total = lax.optimization_barrier(jnp.sum(weights, axis=2))
        rounded = lax.optimization_barrier(weights.astype(jnp.bfloat16)).astype(jnp.float32)
        mixed = jnp.einsum('qhk,khd->qhd', rounded, value_one.astype(jnp.float32))
        return (mixed / total[..., None]).astype(jnp.bfloat16)
    attended = lax.map(attend, (queries, key_rows, value_rows)).reshape(row_total, model_width)
    mixed_out = jnp.dot(attended, w_out, preferred_element_type=jnp.float32)
    hidden_out = (flat_rows.astype(jnp.float32) + mixed_out).astype(jnp.bfloat16)
    spin_all = jnp.broadcast_to(spin[None, :], (walkers, electrons)).reshape(row_total)
    spin_up = (spin_all == 1)[:, None]
    orbitals = jnp.where(spin_up, jnp.dot(hidden_out, w_orb[1], preferred_element_type=jnp.float32), jnp.dot(hidden_out, w_orb[0], preferred_element_type=jnp.float32))
    residual = orbitals - target.reshape(row_total, target.shape[2]).astype(jnp.float32)
    rows_float = jnp.float32(row_total)
    loss = 0.5 * jnp.sum(residual * residual) / rows_float
    signal = residual.astype(jnp.bfloat16)
    zeros_rows = jnp.zeros_like(hidden_out)
    split_rows = jnp.concatenate([jnp.where(spin_up, zeros_rows, hidden_out), jnp.where(spin_up, hidden_out, zeros_rows)], axis=1)
    grad_orb = lax.dot_general(split_rows, signal, (((0,), (0,)), ((), ())), preferred_element_type=jnp.float32) / rows_float
    backward = jnp.where(spin_up, lax.dot_general(signal, w_orb[1], (((1,), (1,)), ((), ())), preferred_element_type=jnp.float32), lax.dot_general(signal, w_orb[0], (((1,), (1,)), ((), ())), preferred_element_type=jnp.float32)).astype(jnp.bfloat16)
    grad_out = lax.dot_general(attended, backward, (((0,), (0,)), ((), ())), preferred_element_type=jnp.float32) / rows_float
    return (grad_orb.reshape(2, model_width, target.shape[2]), grad_out, jnp.reshape(loss, (1,)))
```

```python
import math

import jax
import jax.numpy as jnp
from jax import lax
from jax.experimental import pallas as pl
from jax.experimental.pallas import tpu as pltpu
from jax.sharding import PartitionSpec as P

HEADS = 16
BLOCK = 64
ATOM_DEV = 25
NEAR = 2
KMAX = 4
SLOT = 32
LANES = 128
WIDE = 256
TILE = 16
FULL = 32700.0
FINE = 64.0
HOP_US = 2.6
CORE_US = 1.0
CHUNK_US = 0.8
VMEM_MIB = 62
F32 = jnp.float32
BF16 = jnp.bfloat16
I16 = jnp.int16
VM = pltpu.VMEM
NT = (((1,), (1,)), ((), ()))


def encode(x):
    top = jnp.maximum(jnp.max(jnp.abs(x), axis=0, keepdims=True), 1e-30)
    level = jnp.ceil(jnp.log(top) * (FINE / math.log(2.0)))
    scale = jnp.exp2(level * (-1.0 / FINE)) * FULL
    return jnp.round(x * scale).astype(jnp.int32).astype(I16), level


def unit(level):
    return jnp.exp2(level * (1.0 / FINE)) * (1.0 / FULL)


def widen(codes):
    return codes.astype(jnp.int32).astype(F32)


def layout(piece, tail, blocks):
    plain, coded = [], []
    for c in range(blocks):
        plain.append((c * piece, piece, 0))
        coded.append((c * (piece + TILE), piece + TILE))
    plain.append((blocks * piece, 2 * tail, TILE))
    coded.append((blocks * (piece + TILE), 2 * tail + 2 * TILE))
    return plain, coded


def make_steps(pairs, walks, plain, coded, result, part, out, r1, s2, r2, a2, sz, r3, r4, *sems):
    final_sem = sems[-1]
    send_core, recv_core, send_y, recv_y, send_z, recv_z, send_c, recv_c, send_b, recv_b = sems[:10]
    send_y2, recv_y2, send_core2, recv_core2 = sems[10:14]
    chunks = len(plain)
    finals = []
    elec = lax.axis_index("elec")
    wk = lax.axis_index("walk")
    core, y = lax.rem(elec, 2), elec // 2
    mesh_id = pl.DeviceIdType.MESH
    middle = walks // 2
    on_left = wk < middle
    level = jnp.where(on_left, wk, walks - 1 - wk)
    toward = jnp.where(on_left, 1, walks - 1)
    partner = {"elec": y * 2 + 1 - core}
    inward = {"walk": lax.rem(wk + toward, walks)}
    outward = {"walk": lax.rem(wk + walks - toward, walks)}
    inner_level = middle - 1

    def over_y(k):
        return {"elec": lax.rem(y + 1 + k, pairs) * 2 + core}

    def route(src, dst, ssem, rsem, peer):
        return pltpu.make_async_remote_copy(
            src_ref=src,
            dst_ref=dst,
            send_sem=ssem,
            recv_sem=rsem,
            device_id=peer,
            device_id_type=mesh_id,
        )

    def copies(c):
        low, size, extra = plain[c]
        rng = pl.ds(low, size + extra)
        code = pl.ds(*coded[c])
        whole = out.at[core, :, code]
        mine = out.at[core, y, code]
        return dict(
            core=route(
                part.at[1 - core, :, rng], r1.at[:, rng], send_core.at[c], recv_core.at[c], partner
            ),
            y=[
                route(s2.at[k, code], r2.at[k, code], send_y.at[c, k], recv_y.at[c, k], over_y(k))
                for k in range(pairs - 1)
            ],
            z=route(sz.at[code], r3.at[code], send_z.at[c], recv_z.at[c], inward),
            c=route(sz.at[code], r4.at[code], send_c.at[c], recv_c.at[c], inward),
            b=route(mine, mine, send_b.at[c], recv_b.at[c], outward),
            y2=[
                route(mine, mine, send_y2.at[c, k], recv_y2.at[c, k], over_y(k))
                for k in range(pairs - 1)
            ],
            core2=route(whole, whole, send_core2.at[c], recv_core2.at[c], partner),
        )

    flights = [copies(c) for c in range(chunks)]

    def spans(c):
        low, size, extra = plain[c]
        start = coded[c][0]
        groups = [(pl.ds(low, size), pl.ds(start, size))]
        if extra:
            groups.append((pl.ds(low + size, extra), pl.ds(start + size, extra)))
        return groups, pl.ds(start + size + extra, TILE)

    def code_into(c, read, dst):
        groups, scales = spans(c)
        row = lax.broadcasted_iota(jnp.int32, (TILE, LANES), 0)
        marks = None
        for g, (rows, codes) in enumerate(groups):
            body, mark = encode(read(rows))
            dst[codes] = body
            mark = jnp.broadcast_to(mark, (TILE, LANES))
            marks = mark if marks is None else jnp.where(row < TILE // 2, marks, mark)
        dst[scales] = marks.astype(jnp.int32).astype(I16)

    def decoded(c, src):
        groups, scales = spans(c)
        marks = widen(src[scales])
        return [
            (rows, widen(src[codes]) * unit(marks[g * (TILE // 2) : g * (TILE // 2) + 1]))
            for g, (rows, codes) in enumerate(groups)
        ]

    def send_inward(c, key):
        code_into(c, lambda rows: a2[rows], sz)
        flights[c][key].start()

    def pair_done(c):
        flight = flights[c]
        low, size, extra = plain[c]
        rng = pl.ds(low, size + extra)
        flight["core"].wait_recv()
        for k in range(pairs - 1):
            other = lax.rem(y + 1 + k, pairs)
            code_into(c, lambda rows: r1[other, rows] + part[core, other, rows], s2.at[k])
            flight["y"][k].start()
        a2[rng] = r1[y, rng] + part[core, y, rng]

    def step(stage, c):
        flight = flights[c]
        if stage == 0:
            for k, copy in enumerate(flight["y"]):
                copy.wait_recv()
                for rows, value in decoded(c, r2.at[k]):
                    a2[rows] = a2[rows] + value

            if inner_level > 0:

                @pl.when(level == 0)
                def _():
                    send_inward(c, "z")

        elif stage < middle:

            @pl.when(level == stage)
            def _():
                flight["z"].wait_recv()
                for rows, value in decoded(c, r3):
                    a2[rows] = a2[rows] + value
                if stage < inner_level:
                    send_inward(c, "z")

        if stage == inner_level:

            @pl.when(level == inner_level)
            def _():
                send_inward(c, "c")

        back = stage - middle
        if back == 0:

            @pl.when(level == inner_level)
            def _():
                own = decoded(c, sz)
                flight["c"].wait_recv()
                for (rows, value), (_, other) in zip(own, decoded(c, r4)):
                    a2[rows] = value + other
                code_into(c, lambda rows: a2[rows], out.at[core, y])
                if inner_level > 0:
                    flight["b"].start()
                for copy in flight["y2"]:
                    copy.start()
        elif 0 < back < middle:

            @pl.when(level == inner_level - back)
            def _():
                flight["b"].wait_recv()
                if back < inner_level:
                    flight["b"].start()
                for copy in flight["y2"]:
                    copy.start()

        if back == middle:
            for copy in flight["y2"]:
                copy.wait_recv()
            flight["core2"].start()
            write(c, core)
        elif back == middle + 1:
            flight["core2"].wait_recv()
            write(c, 1 - core)

    def write(c, side):
        code = pl.ds(*coded[c])
        copy = pltpu.make_async_copy(
            out.at[side, :, code], result.at[side, :, code], final_sem.at[len(finals)]
        )
        copy.start()
        finals.append(copy)

    def begin(c):
        flights[c]["core"].start()

    stages = 2 * middle + 2

    def after(done):
        events = [(t, -1, c) for c, t in enumerate(done)]
        ready = list(done)
        for stage in range(stages):
            wait = CORE_US if stage == stages - 1 else HOP_US
            before = -1e9
            for c in range(chunks):
                before = max(ready[c] + wait, before + CHUNK_US)
                ready[c] = before
                events.append((before, stage, c))
        return sorted(events)

    def drain():
        for copy in finals:
            copy.wait()
        for flight in flights:
            for copy in [flight["core"], flight["core2"]] + flight["y"] + flight["y2"]:
                copy.wait_send()

            @pl.when(level < inner_level)
            def _():
                flight["z"].wait_send()

            @pl.when(level == inner_level)
            def _():
                flight["c"].wait_send()

            @pl.when(level > 0)
            def _():
                flight["b"].wait_send()

    return begin, pair_done, step, after, drain


def step_kernel(
    count,
    walks,
    near,
    pairs,
    pair_n,
    emb,
    pos,
    epos,
    spin,
    *rest,
):
    outer, result, inner = rest[:7], rest[7], rest[8:]
    gemb, gpos, gep, gsp = inner[:4]
    held = inner[4:11]
    spin_emb, w_query, w_key, w_value, w_out, w_orb, target = held
    send, recv, local_sem = inner[11:14]
    pstack, estack, e_s, q_s, k_s, vt_s, h_s, bias_s, att_s, part, out = inner[14:25]
    me = lax.axis_index("elec")
    barrier = pltpu.get_barrier_semaphore()
    for k in range(count - 1):
        pl.semaphore_signal(
            barrier,
            inc=1,
            device_id={"elec": lax.rem(me + 1 + k, count)},
            device_id_type=pl.DeviceIdType.MESH,
        )
    wk = lax.axis_index("walk")

    @pl.when(wk > 0)
    def _():
        pl.semaphore_signal(
            barrier,
            inc=1,
            device_id={"walk": lax.rem(wk + walks - 1, walks)},
            device_id_type=pl.DeviceIdType.MESH,
        )

    @pl.when(wk < walks - 1)
    def _():
        pl.semaphore_signal(
            barrier,
            inc=1,
            device_id={"walk": lax.rem(wk + 1, walks)},
            device_id_type=pl.DeviceIdType.MESH,
        )

    ends = jnp.where(wk > 0, 1, 0) + jnp.where(wk < walks - 1, 1, 0)
    small = ((emb, gemb), (pos, gpos), (epos, gep), (spin, gsp))
    own = [
        pltpu.make_async_copy(src, dst.at[me], local_sem.at[i])
        for i, (src, dst) in enumerate(small)
    ]
    loads = [
        pltpu.make_async_copy(src, dst, local_sem.at[4 + i])
        for i, (src, dst) in enumerate(zip(outer, held))
    ]
    for copy in own + loads:
        copy.start()
    pl.semaphore_wait(barrier, count - 1 + ends)
    copies = []
    for k in range(count - 1):
        for i, (src, dst) in enumerate(small):
            copy = pltpu.make_async_remote_copy(
                src_ref=src,
                dst_ref=dst.at[me],
                send_sem=send.at[k, i],
                recv_sem=recv.at[k, i],
                device_id={"elec": lax.rem(me + 1 + k, count)},
                device_id_type=pl.DeviceIdType.MESH,
            )
            copy.start()
            copies.append(copy)
    walkers, rows = gep.shape[2], gep.shape[3]
    width = w_query.shape[0]
    head = width // HEADS
    per_device = rows // BLOCK
    owners = (me, lax.rem(me + count - 1, count), lax.rem(me + 1, count))
    pstack[...] = jnp.zeros_like(pstack)
    estack[...] = jnp.zeros_like(estack)
    e_s[...] = jnp.zeros_like(e_s)
    depth = per_device * NEAR * SLOT
    row_id = lax.broadcasted_iota(jnp.int32, (rows, depth), 0)
    lane_id = lax.broadcasted_iota(jnp.int32, (rows, depth), 1)
    block_mask = (row_id // BLOCK) == (lane_id // (NEAR * SLOT))
    half_lane = lax.broadcasted_iota(jnp.int32, (BLOCK, 2 * rows), 1)
    for j, owner in enumerate(owners):
        for kb in range(per_device):
            key_block = owner * per_device + kb
            value = jnp.zeros((BLOCK, 2 * rows), F32)
            for p in range(per_device):
                query_block = me * per_device + p
                listed = None
                for slot in range(KMAX):
                    hit = jnp.logical_and(
                        pairs[slot, query_block] == key_block, slot < pair_n[0, query_block]
                    )
                    listed = hit if listed is None else jnp.logical_or(listed, hit)
                level = jnp.where(listed, 0.0, -1e30).astype(F32)
                value = jnp.where(half_lane % rows // BLOCK == p, level, value)
            start = j * rows + kb * BLOCK
            bias_s[start : start + BLOCK, :] = value
    for copy in own + loads[:4]:
        copy.wait()
    wv_t = w_value[...].astype(F32).T.astype(BF16)
    for copy in copies:
        copy.wait_recv()
    spin_cols = []
    for j, owner in enumerate(owners):
        for p in range(per_device):
            for n in range(NEAR):
                slot = p * NEAR + n
                group = near[n, owner * per_device + p]
                pstack[j, 0:3, slot * SLOT : slot * SLOT + ATOM_DEV] = gpos[group]
                estack[j, slot * SLOT : slot * SLOT + ATOM_DEV, :] = gemb[group]
        estack[j, ATOM_DEV : ATOM_DEV + 2, :] = spin_emb[...]
        electron = gep[owner]
        for axis in range(3):
            e_s[j, axis * walkers : (axis + 1) * walkers, :] = electron[axis]
        e_s[j, 3 * walkers : 3 * walkers + 1, :] = gsp[owner].astype(F32)
        columns = e_s[j].T
        up_one = columns[:, 3 * walkers : 3 * walkers + 1]
        spin_cols.append(up_one)
        pieces = []
        for w in range(walkers):
            distance = jnp.zeros((rows, depth), F32)
            for axis in range(3):
                at = axis * walkers + w
                spacing = columns[:, at : at + 1] - pstack[j, axis : axis + 1, :]
                distance = distance + spacing * spacing
            close = jnp.where(block_mask, 1.0 / (1.0 + distance), 0.0)
            close = jnp.where(lane_id == ATOM_DEV, 1.0 - up_one, close)
            close = jnp.where(lane_id == ATOM_DEV + 1, up_one, close)
            pieces.append(close)
        close_all = jnp.concatenate(pieces, axis=0)
        hidden = jnp.dot(
            close_all,
            estack[j],
            precision=lax.Precision.HIGHEST,
            preferred_element_type=F32,
        ).astype(BF16)
        keys = jnp.dot(hidden, w_key[...], preferred_element_type=F32).astype(BF16)
        values_t = lax.dot_general(wv_t, hidden, NT, preferred_element_type=F32).astype(BF16)
        for w in range(walkers):
            k_s[w, j * rows : (j + 1) * rows, :] = keys[w * rows : (w + 1) * rows]
            vt_s[w, :, j * rows : (j + 1) * rows] = values_t[:, w * rows : (w + 1) * rows]
        if j == 0:
            h_s[...] = hidden
            queries = jnp.dot(hidden, w_query[...], preferred_element_type=F32).astype(BF16)
            queries = queries.astype(F32) * (1.0 / math.sqrt(head))
            for w in range(walkers):
                q_s[w] = queries[w * rows : (w + 1) * rows]
    head_lane = lax.broadcasted_iota(jnp.int32, (rows, width), 1) // head

    def walker(w, carry):
        query = q_s[w]
        key = k_s[w]
        for pair in range(HEADS // 2):
            both = jnp.concatenate(
                [
                    jnp.where(head_lane == 2 * pair, query, 0.0),
                    jnp.where(head_lane == 2 * pair + 1, query, 0.0),
                ],
                axis=0,
            ).astype(BF16)
            scores = lax.dot_general(key, both, NT, preferred_element_type=F32) + bias_s[...]
            top = jnp.max(scores, axis=0, keepdims=True)
            weights = jnp.exp(scores - top)
            total = jnp.sum(weights, axis=0, keepdims=True)
            mixed = jnp.dot(
                vt_s[w, 2 * pair * head : 2 * (pair + 1) * head, :],
                weights.astype(BF16),
                preferred_element_type=F32,
            )
            mixed = mixed / total
            att_s[w, 2 * pair * head : (2 * pair + 1) * head, :] = mixed[:head, :rows]
            att_s[w, (2 * pair + 1) * head : 2 * (pair + 1) * head, :] = mixed[head:, rows:]
        return carry

    lax.fori_loop(0, walkers, walker, 0)
    for copy in loads[4:]:
        copy.wait()
    att_t = jnp.concatenate([att_s[w].astype(BF16) for w in range(walkers)], axis=1)
    attended = jnp.concatenate([att_s[w].T for w in range(walkers)], axis=0).astype(BF16)
    mixed_out = jnp.dot(attended, w_out[...], preferred_element_type=F32)
    hidden_out = (h_s[...].astype(F32) + mixed_out).astype(BF16).astype(F32)
    spin_row = gsp[me].astype(F32)
    spin_col = spin_cols[0]
    up_col = jnp.concatenate([spin_col] * walkers, axis=0) > 0.5
    up_lane = jnp.concatenate([spin_row] * walkers, axis=1) > 0.5
    split = jnp.concatenate(
        [jnp.where(up_col, 0.0, hidden_out), jnp.where(up_col, hidden_out, 0.0)], axis=1
    ).astype(BF16)
    hidden_t = hidden_out.T
    split_t = jnp.concatenate(
        [jnp.where(up_lane, 0.0, hidden_t), jnp.where(up_lane, hidden_t, 0.0)], axis=0
    ).astype(BF16)
    orbitals = target.shape[1]
    both_rows = 2 * width
    pairs = count // 2
    piece = both_rows // count
    tail = width // count
    blocks = orbitals // LANES
    plain, coded = layout(piece, tail, blocks)
    begin, pair_done, step, after, drain = make_steps(
        pairs, walks, plain, coded, result, part, out, *inner[25:]
    )
    share = 1.0 / (walkers * rows * count * lax.axis_size("walk"))
    backward = None
    loss = jnp.zeros((1, WIDE), F32)
    halves = WIDE // LANES
    for c in range(orbitals // WIDE):
        columns = slice(c * WIDE, (c + 1) * WIDE)
        w_piece = w_orb[:, columns]
        residual = jnp.dot(split, w_piece, preferred_element_type=F32) - target[
            :, columns
        ].astype(F32)
        loss = loss + jnp.sum(residual * residual, axis=0, keepdims=True)
        signal = residual.astype(BF16)
        grad = share * jnp.dot(split_t, signal, preferred_element_type=F32)
        for h in range(halves):
            low = plain[halves * c + h][0]
            for q in range(count):
                part[q // pairs, q % pairs, low : low + piece, :] = grad[
                    q * piece : (q + 1) * piece, h * LANES : (h + 1) * LANES
                ]
            begin(halves * c + h)
        if c > 0:
            for h in range(halves):
                pair_done(halves * (c - 1) + h)
        term = lax.dot_general(signal, w_piece, NT, preferred_element_type=F32)
        backward = term if backward is None else backward + term
    chosen = jnp.where(up_col, backward[:, width:], backward[:, :width]).astype(BF16)
    grad = share * jnp.dot(att_t, chosen, preferred_element_type=F32)
    spread = (0.5 * share) * jnp.sum(loss, axis=1, keepdims=True)
    base = plain[-1][0]
    for q in range(count):
        here = part.at[q // pairs, q % pairs]
        for h in range(halves):
            here[base + h * tail : base + (h + 1) * tail, :] = grad[
                q * tail : (q + 1) * tail, h * LANES : (h + 1) * LANES
            ]
        here[base + halves * tail : base + halves * tail + TILE, :] = jnp.broadcast_to(
            spread, (TILE, LANES)
        )
    begin(blocks)
    early = blocks - halves
    done = [(c // halves) * 0.7 - 2.0 if c < early else 0.3 * (c - early) for c in range(blocks + 1)]
    for _, stage, c in after(done):
        if stage >= 0:
            step(stage, c)
        elif c >= early:
            pair_done(c)
    drain()
    for copy in copies:
        copy.wait_send()


def plain_kernel(plain, coded, codes, g_orb, g_out, g_loss):
    for c, ((_, size, extra), (start, length)) in enumerate(zip(plain, coded)):
        marks = widen(codes[start + size + extra : start + length])
        value = widen(codes[start : start + size]) * unit(marks[:1])
        if not extra:
            g_orb[:, c * LANES : (c + 1) * LANES] = value
            continue
        tail = g_out.shape[0]
        for h in range(g_out.shape[1] // LANES):
            g_out[:, h * LANES : (h + 1) * LANES] = value[h * tail : (h + 1) * tail]
        sums = widen(codes[start + size : start + size + extra]) * unit(marks[TILE // 2 : TILE // 2 + 1])
        g_loss[0] = jnp.max(sums)


def local(
    elec_pos,
    atom_pos,
    atom_emb,
    spin_emb,
    spin,
    near_atoms,
    pair_list,
    pair_count,
    w_query,
    w_key,
    w_value,
    w_out,
    w_orb,
    target,
):
    walkers, rows = elec_pos.shape[1], elec_pos.shape[2]
    count, walks = lax.axis_size("elec"), lax.axis_size("walk")
    width, orbitals = w_query.shape[0], w_orb.shape[2]
    row_local = walkers * rows
    smem = pl.BlockSpec(memory_space=pltpu.SMEM)
    sem = pltpu.SemaphoreType.DMA
    hbm = pl.BlockSpec(memory_space=pltpu.HBM)
    pairs = count // 2
    plain, coded = layout(2 * width // count, width // count, orbitals // LANES)
    chunks = len(plain)
    height = sum(plain[-1])
    long = sum(coded[-1])
    one, many = sem((chunks,)), sem((chunks, pairs - 1))
    depth = rows // BLOCK * NEAR * SLOT
    codes = pl.pallas_call(
        lambda *refs: step_kernel(count, walks, *refs),
        out_shape=jax.ShapeDtypeStruct((2, pairs, long, LANES), I16),
        in_specs=[smem] * 3 + [hbm] * 11,
        out_specs=hbm,
        scratch_shapes=[
            VM((count, ATOM_DEV, width), F32),
            VM((count, 3, ATOM_DEV), F32),
            VM((count, 3, walkers, rows), F32),
            VM((count, 1, rows), jnp.int32),
            VM((2, width), F32),
            VM((width, width), BF16),
            VM((width, width), BF16),
            VM((width, width), BF16),
            VM((width, width), BF16),
            VM((2 * width, orbitals), BF16),
            VM((row_local, orbitals), BF16),
            sem((count - 1, 4)),
            sem((count - 1, 4)),
            sem((11,)),
            VM((3, 8, depth), F32),
            VM((3, depth, width), F32),
            VM((3, rows, rows), F32),
            VM((walkers, rows, width), F32),
            VM((walkers, 3 * rows, width), BF16),
            VM((walkers, width, 3 * rows), BF16),
            VM((row_local, width), BF16),
            VM((3 * rows, 2 * rows), F32),
            VM((walkers, width, rows), F32),
            VM((2, pairs, height, LANES), F32),
            VM((2, pairs, long, LANES), I16),
            VM((pairs, height, LANES), F32),
            VM((pairs - 1, long, LANES), I16),
            VM((pairs - 1, long, LANES), I16),
            VM((height, LANES), F32),
            VM((long, LANES), I16),
            VM((long, LANES), I16),
            VM((long, LANES), I16),
        ]
        + [one] * 2
        + [many] * 2
        + [one] * 6
        + [many] * 2
        + [one] * 2
        + [sem((2 * chunks,))],
        compiler_params=pltpu.CompilerParams(
            collective_id=0, has_side_effects=True, vmem_limit_bytes=VMEM_MIB * 1024 * 1024
        ),
        name="whole_step",
    )(
        near_atoms.T,
        pair_list.T,
        pair_count.reshape(1, -1),
        atom_emb,
        atom_pos.T,
        elec_pos,
        spin.reshape(1, rows),
        spin_emb,
        w_query,
        w_key,
        w_value,
        w_out,
        w_orb.reshape(2 * width, orbitals),
        target.reshape(row_local, orbitals),
    )
    piece, tail = 2 * width // count, width // count
    grad_orb, grad_out, loss = pl.pallas_call(
        lambda *refs: plain_kernel(plain, coded, *refs),
        grid=(count,),
        out_shape=(
            jax.ShapeDtypeStruct((2 * width, orbitals), F32),
            jax.ShapeDtypeStruct((width, width), F32),
            jax.ShapeDtypeStruct((1,), F32),
        ),
        in_specs=[pl.BlockSpec((None, None, long, LANES), lambda q: (q // pairs, q % pairs, 0, 0))],
        out_specs=(
            pl.BlockSpec((piece, orbitals), lambda q: (q, 0)),
            pl.BlockSpec((tail, width), lambda q: (q, 0)),
            smem,
        ),
        name="decode",
    )(codes)
    return (grad_orb.reshape(2, width, orbitals), grad_out, loss)


def solution(mesh):
    in_specs = (
        P(None, ("parts", "walk"), "elec"),
        P(("parts", "elec"), None),
        P(("parts", "elec"), None),
        P(),
        P(("parts", "elec")),
        P("parts", None),
        P("parts", None),
        P("parts"),
        P(),
        P(),
        P(),
        P(),
        P(),
        P(("parts", "walk"), "elec", None),
    )
    out_specs = (P("parts", None, None), P("parts", None), P("parts"))
    return jax.shard_map(local, mesh=mesh, in_specs=in_specs, out_specs=out_specs, check_vma=False)
```

```python
import math

import jax
import jax.numpy as jnp
from jax import lax
from jax.experimental import pallas as pl
from jax.experimental.pallas import tpu as pltpu
from jax.sharding import PartitionSpec as P

HEADS = 16
BLOCK = 64
ATOM_DEV = 25
NEAR = 2
KMAX = 4
SLOT = 32
LANES = 128
WIDE = 256
TILE = 16
FULL = 32700.0
FINE = 64.0
HOP_US = 2.0
CORE_US = 1.0
CHUNK_US = 0.4
VMEM_MIB = 62
F32 = jnp.float32
BF16 = jnp.bfloat16
I16 = jnp.int16
VM = pltpu.VMEM
NT = (((1,), (1,)), ((), ()))


def encode(x):
    top = jnp.maximum(jnp.max(jnp.abs(x), axis=0, keepdims=True), 1e-30)
    level = jnp.ceil(jnp.log(top) * (FINE / math.log(2.0)))
    scale = jnp.exp2(level * (-1.0 / FINE)) * FULL
    return jnp.round(x * scale).astype(jnp.int32).astype(I16), level


def unit(level):
    return jnp.exp2(level * (1.0 / FINE)) * (1.0 / FULL)


def widen(codes):
    return codes.astype(jnp.int32).astype(F32)


def layout(piece, tail, blocks):
    plain, coded = [], []
    for c in range(blocks):
        plain.append((c * piece, piece, 0))
        coded.append((c * (piece + TILE), piece + TILE))
    plain.append((blocks * piece, 2 * tail, TILE))
    coded.append((blocks * (piece + TILE), 2 * tail + 2 * TILE))
    return plain, coded


def make_steps(pairs, walks, plain, coded, result, part, out, r1, s2, r2, a2, sz, r3, r4, *sems):
    final_sem = sems[-1]
    send_core, recv_core, send_y, recv_y, send_z, recv_z, send_c, recv_c, send_b, recv_b = sems[:10]
    send_y2, recv_y2, send_core2, recv_core2 = sems[10:14]
    chunks = len(plain)
    finals = []
    elec = lax.axis_index("elec")
    wk = lax.axis_index("walk")
    core, y = lax.rem(elec, 2), elec // 2
    mesh_id = pl.DeviceIdType.MESH
    middle = walks // 2
    on_left = wk < middle
    level = jnp.where(on_left, wk, walks - 1 - wk)
    toward = jnp.where(on_left, 1, walks - 1)
    partner = {"elec": y * 2 + 1 - core}
    inward = {"walk": lax.rem(wk + toward, walks)}
    outward = {"walk": lax.rem(wk + walks - toward, walks)}
    inner_level = middle - 1

    def over_y(k):
        return {"elec": lax.rem(y + 1 + k, pairs) * 2 + core}

    def route(src, dst, ssem, rsem, peer):
        return pltpu.make_async_remote_copy(
            src_ref=src,
            dst_ref=dst,
            send_sem=ssem,
            recv_sem=rsem,
            device_id=peer,
            device_id_type=mesh_id,
        )

    def copies(c):
        low, size, extra = plain[c]
        rng = pl.ds(low, size + extra)
        code = pl.ds(*coded[c])
        whole = out.at[core, :, code]
        mine = out.at[core, y, code]
        return dict(
            core=route(
                part.at[1 - core, :, rng], r1.at[:, rng], send_core.at[c], recv_core.at[c], partner
            ),
            y=[
                route(s2.at[k, code], r2.at[k, code], send_y.at[c, k], recv_y.at[c, k], over_y(k))
                for k in range(pairs - 1)
            ],
            z=route(sz.at[code], r3.at[code], send_z.at[c], recv_z.at[c], inward),
            c=route(sz.at[code], r4.at[code], send_c.at[c], recv_c.at[c], inward),
            b=route(mine, mine, send_b.at[c], recv_b.at[c], outward),
            y2=[
                route(mine, mine, send_y2.at[c, k], recv_y2.at[c, k], over_y(k))
                for k in range(pairs - 1)
            ],
            core2=route(whole, whole, send_core2.at[c], recv_core2.at[c], partner),
        )

    flights = [copies(c) for c in range(chunks)]

    def spans(c):
        low, size, extra = plain[c]
        start = coded[c][0]
        groups = [(pl.ds(low, size), pl.ds(start, size))]
        if extra:
            groups.append((pl.ds(low + size, extra), pl.ds(start + size, extra)))
        return groups, pl.ds(start + size + extra, TILE)

    def code_into(c, read, dst):
        groups, scales = spans(c)
        row = lax.broadcasted_iota(jnp.int32, (TILE, LANES), 0)
        marks = None
        for g, (rows, codes) in enumerate(groups):
            body, mark = encode(read(rows))
            dst[codes] = body
            mark = jnp.broadcast_to(mark, (TILE, LANES))
            marks = mark if marks is None else jnp.where(row < TILE // 2, marks, mark)
        dst[scales] = marks.astype(jnp.int32).astype(I16)

    def decoded(c, src):
        groups, scales = spans(c)
        marks = widen(src[scales])
        return [
            (rows, widen(src[codes]) * unit(marks[g * (TILE // 2) : g * (TILE // 2) + 1]))
            for g, (rows, codes) in enumerate(groups)
        ]

    def send_inward(c, key):
        code_into(c, lambda rows: a2[rows], sz)
        flights[c][key].start()

    def pair_done(c):
        flight = flights[c]
        low, size, extra = plain[c]
        rng = pl.ds(low, size + extra)
        flight["core"].wait_recv()
        for k in range(pairs - 1):
            other = lax.rem(y + 1 + k, pairs)
            code_into(c, lambda rows: r1[other, rows] + part[core, other, rows], s2.at[k])
            flight["y"][k].start()
        a2[rng] = r1[y, rng] + part[core, y, rng]

    def step(stage, c):
        flight = flights[c]
        if stage == 0:
            for k, copy in enumerate(flight["y"]):
                copy.wait_recv()
                for rows, value in decoded(c, r2.at[k]):
                    a2[rows] = a2[rows] + value

            if inner_level > 0:

                @pl.when(level == 0)
                def _():
                    send_inward(c, "z")

        elif stage < middle:

            @pl.when(level == stage)
            def _():
                flight["z"].wait_recv()
                for rows, value in decoded(c, r3):
                    a2[rows] = a2[rows] + value
                if stage < inner_level:
                    send_inward(c, "z")

        if stage == inner_level:

            @pl.when(level == inner_level)
            def _():
                send_inward(c, "c")

        back = stage - middle
        if back == 0:

            @pl.when(level == inner_level)
            def _():
                own = decoded(c, sz)
                flight["c"].wait_recv()
                for (rows, value), (_, other) in zip(own, decoded(c, r4)):
                    a2[rows] = value + other
                code_into(c, lambda rows: a2[rows], out.at[core, y])
                if inner_level > 0:
                    flight["b"].start()
                for copy in flight["y2"]:
                    copy.start()
        elif 0 < back < middle:

            @pl.when(level == inner_level - back)
            def _():
                flight["b"].wait_recv()
                if back < inner_level:
                    flight["b"].start()
                for copy in flight["y2"]:
                    copy.start()

        if back == middle:
            for copy in flight["y2"]:
                copy.wait_recv()
            flight["core2"].start()
            write(c, core)
        elif back == middle + 1:
            flight["core2"].wait_recv()
            write(c, 1 - core)

    def write(c, side):
        code = pl.ds(*coded[c])
        copy = pltpu.make_async_copy(
            out.at[side, :, code], result.at[side, :, code], final_sem.at[len(finals)]
        )
        copy.start()
        finals.append(copy)

    def begin(c):
        flights[c]["core"].start()

    stages = 2 * middle + 2

    def after(done):
        events = [(t, -1, c) for c, t in enumerate(done)]
        ready = list(done)
        for stage in range(stages):
            wait = CORE_US if stage == stages - 1 else HOP_US
            before = -1e9
            for c in range(chunks):
                before = max(ready[c] + wait, before + CHUNK_US)
                ready[c] = before
                events.append((before, stage, c))
        return sorted(events)

    def drain():
        for copy in finals:
            copy.wait()
        for flight in flights:
            for copy in [flight["core"], flight["core2"]] + flight["y"] + flight["y2"]:
                copy.wait_send()

            @pl.when(level < inner_level)
            def _():
                flight["z"].wait_send()

            @pl.when(level == inner_level)
            def _():
                flight["c"].wait_send()

            @pl.when(level > 0)
            def _():
                flight["b"].wait_send()

    return begin, pair_done, step, after, drain


def step_kernel(
    count,
    walks,
    near,
    pairs,
    pair_n,
    emb,
    pos,
    epos,
    spin,
    *rest,
):
    outer, result, inner = rest[:7], rest[7], rest[8:]
    gemb, gpos, gep, gsp = inner[:4]
    held = inner[4:11]
    spin_emb, w_query, w_key, w_value, w_out, w_orb, target = held
    send, recv, local_sem = inner[11:14]
    pstack, estack, e_s, q_s, v_s, kt_s, h_s, att_s, part, out = inner[14:24]
    me = lax.axis_index("elec")
    barrier = pltpu.get_barrier_semaphore()
    for k in range(count - 1):
        pl.semaphore_signal(
            barrier,
            inc=1,
            device_id={"elec": lax.rem(me + 1 + k, count)},
            device_id_type=pl.DeviceIdType.MESH,
        )
    wk = lax.axis_index("walk")

    @pl.when(wk > 0)
    def _():
        pl.semaphore_signal(
            barrier,
            inc=1,
            device_id={"walk": lax.rem(wk + walks - 1, walks)},
            device_id_type=pl.DeviceIdType.MESH,
        )

    @pl.when(wk < walks - 1)
    def _():
        pl.semaphore_signal(
            barrier,
            inc=1,
            device_id={"walk": lax.rem(wk + 1, walks)},
            device_id_type=pl.DeviceIdType.MESH,
        )

    ends = jnp.where(wk > 0, 1, 0) + jnp.where(wk < walks - 1, 1, 0)
    small = ((emb, gemb), (pos, gpos), (epos, gep), (spin, gsp))
    own = [
        pltpu.make_async_copy(src, dst.at[me], local_sem.at[i])
        for i, (src, dst) in enumerate(small)
    ]
    loads = [
        pltpu.make_async_copy(src, dst, local_sem.at[4 + i])
        for i, (src, dst) in enumerate(zip(outer, held))
    ]
    for copy in own + loads:
        copy.start()
    pl.semaphore_wait(barrier, count - 1 + ends)
    copies = []
    for k in range(count - 1):
        for i, (src, dst) in enumerate(small):
            copy = pltpu.make_async_remote_copy(
                src_ref=src,
                dst_ref=dst.at[me],
                send_sem=send.at[k, i],
                recv_sem=recv.at[k, i],
                device_id={"elec": lax.rem(me + 1 + k, count)},
                device_id_type=pl.DeviceIdType.MESH,
            )
            copy.start()
            copies.append(copy)
    walkers, rows = gep.shape[2], gep.shape[3]
    width = w_query.shape[0]
    head = width // HEADS
    per_device = rows // BLOCK
    owners = (me, lax.rem(me + count - 1, count), lax.rem(me + 1, count))
    pstack[...] = jnp.zeros_like(pstack)
    estack[...] = jnp.zeros_like(estack)
    e_s[...] = jnp.zeros_like(e_s)
    depth = per_device * NEAR * SLOT
    first_half = lax.broadcasted_iota(jnp.int32, (width, 2 * BLOCK), 1) < BLOCK
    row_id = lax.broadcasted_iota(jnp.int32, (rows, depth), 0)
    lane_id = lax.broadcasted_iota(jnp.int32, (rows, depth), 1)
    block_mask = (row_id // BLOCK) == (lane_id // (NEAR * SLOT))
    places, valid = [], []
    for p in range(per_device):
        query_block = me * per_device + p
        for slot in range(KMAX):
            used = slot < pair_n[0, query_block]
            key_block = jnp.where(used, pairs[slot, query_block], query_block)
            away = lax.rem(key_block // per_device - me + count, count)
            side = jnp.where(away == 0, 0, jnp.where(away == 1, 2, 1))
            places.append(side * per_device + lax.rem(key_block, per_device))
            valid.append(jnp.where(used, 1.0, 0.0).astype(F32))
    for copy in own + loads[:4]:
        copy.wait()
    wk_t = w_key[...].astype(F32).T.astype(BF16)
    for copy in copies:
        copy.wait_recv()
    spin_cols = []
    for j, owner in enumerate(owners):
        for p in range(per_device):
            for n in range(NEAR):
                slot = p * NEAR + n
                group = near[n, owner * per_device + p]
                pstack[j, 0:3, slot * SLOT : slot * SLOT + ATOM_DEV] = gpos[group]
                estack[j, slot * SLOT : slot * SLOT + ATOM_DEV, :] = gemb[group]
        estack[j, ATOM_DEV : ATOM_DEV + 2, :] = spin_emb[...]
        electron = gep[owner]
        for axis in range(3):
            e_s[j, axis * walkers : (axis + 1) * walkers, :] = electron[axis]
        e_s[j, 3 * walkers : 3 * walkers + 1, :] = gsp[owner].astype(F32)
        columns = e_s[j].T
        up_one = columns[:, 3 * walkers : 3 * walkers + 1]
        spin_cols.append(up_one)
        pieces = []
        for w in range(walkers):
            distance = jnp.zeros((rows, depth), F32)
            for axis in range(3):
                at = axis * walkers + w
                spacing = columns[:, at : at + 1] - pstack[j, axis : axis + 1, :]
                distance = distance + spacing * spacing
            close = jnp.where(block_mask, 1.0 / (1.0 + distance), 0.0)
            close = jnp.where(lane_id == ATOM_DEV, 1.0 - up_one, close)
            close = jnp.where(lane_id == ATOM_DEV + 1, up_one, close)
            pieces.append(close)
        close_all = jnp.concatenate(pieces, axis=0)
        hidden = jnp.dot(
            close_all,
            estack[j],
            precision=lax.Precision.HIGHEST,
            preferred_element_type=F32,
        ).astype(BF16)
        values = jnp.dot(hidden, w_value[...], preferred_element_type=F32).astype(BF16)
        keys_t = lax.dot_general(wk_t, hidden, NT, preferred_element_type=F32)
        for w in range(walkers):
            across = keys_t[:, w * rows : (w + 1) * rows]
            turned = jnp.concatenate([across[:, BLOCK:], across[:, :BLOCK]], axis=1)
            for p in range(per_device):
                at = j * per_device + p
                start = w * rows + p * BLOCK
                v_s[w, at] = values[start : start + BLOCK]
                both = (across, turned) if p == 0 else (turned, across)
                kt_s[w, at] = jnp.where(first_half, *both).astype(BF16)
        if j == 0:
            h_s[...] = hidden
            queries = jnp.dot(hidden, w_query[...], preferred_element_type=F32).astype(BF16)
            queries = (queries.astype(F32) * (1.0 / math.sqrt(head))).astype(BF16)
            for w in range(walkers):
                for p in range(per_device):
                    start = w * rows + p * BLOCK
                    q_s[w, p] = queries[start : start + BLOCK]
    group = rows // head
    head_lane = lax.broadcasted_iota(jnp.int32, (BLOCK, rows), 1) // head
    head_masks = [jnp.where(head_lane == h, 1.0, 0.0).astype(BF16) for h in range(group)]
    half_row = lax.broadcasted_iota(jnp.int32, (1, 2 * BLOCK), 1) < BLOCK

    def walker(w, carry):
        for p in range(per_device):
            slots = range(p * KMAX, (p + 1) * KMAX)
            values = jnp.concatenate([v_s[w, places[s]] for s in slots], axis=0)
            keys_t = jnp.concatenate(
                [
                    jnp.where(first_half, kt_s[w, places[s]], kt_s[w, places[s + 1]])
                    for s in slots[::2]
                ],
                axis=1,
            )
            allowed = jnp.concatenate(
                [jnp.where(half_row, valid[s], valid[s + 1]) for s in slots[::2]], axis=1
            )
            for low in range(0, width, rows):
                query = q_s[w, p, :, low : low + rows]
                spread = jnp.concatenate([query * mask for mask in head_masks], axis=0)
                scores = jnp.dot(spread, keys_t[low : low + rows], preferred_element_type=F32)
                top = jnp.max(scores, axis=1, keepdims=True)
                weights = jnp.exp(scores - top) * allowed
                total = jnp.sum(weights, axis=1, keepdims=True)
                mixed = jnp.dot(
                    weights.astype(BF16), values[:, low : low + rows], preferred_element_type=F32
                )
                above, below = mixed[:BLOCK], jnp.broadcast_to(total[:BLOCK], (BLOCK, rows))
                for h in range(1, group):
                    mine = slice(h * BLOCK, (h + 1) * BLOCK)
                    above = jnp.where(head_lane == h, mixed[mine], above)
                    below = jnp.where(head_lane == h, total[mine], below)
                att_s[w, p * BLOCK : (p + 1) * BLOCK, low : low + rows] = above / below
        return carry

    lax.fori_loop(0, walkers, walker, 0)
    for copy in loads[4:]:
        copy.wait()
    attended_wide = jnp.concatenate([att_s[w] for w in range(walkers)], axis=0)
    attended = attended_wide.astype(BF16)
    mixed_out = jnp.dot(attended, w_out[...], preferred_element_type=F32)
    hidden_out = (h_s[...].astype(F32) + mixed_out).astype(BF16).astype(F32)
    spin_row = gsp[me].astype(F32)
    spin_col = spin_cols[0]
    up_col = jnp.concatenate([spin_col] * walkers, axis=0) > 0.5
    up_lane = jnp.concatenate([spin_row] * walkers, axis=1) > 0.5
    split = jnp.concatenate(
        [jnp.where(up_col, 0.0, hidden_out), jnp.where(up_col, hidden_out, 0.0)], axis=1
    ).astype(BF16)
    hidden_t = hidden_out.T
    split_t = jnp.concatenate(
        [jnp.where(up_lane, 0.0, hidden_t), jnp.where(up_lane, hidden_t, 0.0)], axis=0
    ).astype(BF16)
    orbitals = target.shape[1]
    both_rows = 2 * width
    pairs = count // 2
    piece = both_rows // count
    tail = width // count
    blocks = orbitals // LANES
    plain, coded = layout(piece, tail, blocks)
    begin, pair_done, step, after, drain = make_steps(
        pairs, walks, plain, coded, result, part, out, *inner[24:]
    )
    share = 1.0 / (walkers * rows * count * lax.axis_size("walk"))
    backward = None
    loss = jnp.zeros((1, WIDE), F32)
    halves = WIDE // LANES
    for c in range(orbitals // WIDE):
        columns = slice(c * WIDE, (c + 1) * WIDE)
        w_piece = w_orb[:, columns]
        residual = jnp.dot(split, w_piece, preferred_element_type=F32) - target[
            :, columns
        ].astype(F32)
        loss = loss + jnp.sum(residual * residual, axis=0, keepdims=True)
        signal = residual.astype(BF16)
        grad = share * jnp.dot(split_t, signal, preferred_element_type=F32)
        for h in range(halves):
            low = plain[halves * c + h][0]
            for q in range(count):
                part[q // pairs, q % pairs, low : low + piece, :] = grad[
                    q * piece : (q + 1) * piece, h * LANES : (h + 1) * LANES
                ]
            begin(halves * c + h)
        if c > 0:
            for h in range(halves):
                pair_done(halves * (c - 1) + h)
        term = lax.dot_general(signal, w_piece, NT, preferred_element_type=F32)
        backward = term if backward is None else backward + term
    chosen = jnp.where(up_col, backward[:, width:], backward[:, :width]).astype(BF16)
    att_t = attended_wide.T.astype(BF16)
    grad = share * jnp.dot(att_t, chosen, preferred_element_type=F32)
    spread = (0.5 * share) * jnp.sum(loss, axis=1, keepdims=True)
    base = plain[-1][0]
    for q in range(count):
        here = part.at[q // pairs, q % pairs]
        for h in range(halves):
            here[base + h * tail : base + (h + 1) * tail, :] = grad[
                q * tail : (q + 1) * tail, h * LANES : (h + 1) * LANES
            ]
        here[base + halves * tail : base + halves * tail + TILE, :] = jnp.broadcast_to(
            spread, (TILE, LANES)
        )
    begin(blocks)
    early = blocks - halves
    done = [(c // halves) * 0.7 - 2.0 if c < early else 0.3 * (c - early) for c in range(blocks + 1)]
    for _, stage, c in after(done):
        if stage >= 0:
            step(stage, c)
        elif c >= early:
            pair_done(c)
    drain()
    for copy in copies:
        copy.wait_send()


def plain_kernel(plain, coded, source, g_orb, g_out, g_loss, codes, orb, low, sems):
    pairs = codes.shape[1]
    count = 2 * pairs
    piece, tail = orb.shape[0] // count, low.shape[0] // count
    copies = []
    loads = []
    for q in range(count):
        at = (q // pairs, q % pairs)
        loads.append(pltpu.make_async_copy(source.at[at], codes.at[at], sems.at[count + 1 + q]))
        loads[-1].start()

    def emit(src, dst):
        copy = pltpu.make_async_copy(src, dst, sems.at[len(copies)])
        copy.start()
        copies.append(copy)

    for q in range(count):
        loads[q].wait()
        here = codes.at[q // pairs, q % pairs]
        rows = slice(q * piece, (q + 1) * piece)
        for c, ((_, size, extra), (start, length)) in enumerate(zip(plain, coded)):
            marks = widen(here[start + size + extra : start + length])
            value = widen(here[start : start + size]) * unit(marks[:1])
            if not extra:
                orb[rows, c * LANES : (c + 1) * LANES] = value
                continue
            for h in range(low.shape[1] // LANES):
                low[q * tail : (q + 1) * tail, h * LANES : (h + 1) * LANES] = value[
                    h * tail : (h + 1) * tail
                ]
        emit(orb.at[rows], g_orb.at[rows])
        if q == 0:
            mark = marks[TILE // 2 : TILE // 2 + 1]
            sums = widen(here[start + size : start + size + extra]) * unit(mark)
            g_loss[0] = jnp.max(sums)
    emit(low, g_out)
    for copy in copies:
        copy.wait()


def local(
    elec_pos,
    atom_pos,
    atom_emb,
    spin_emb,
    spin,
    near_atoms,
    pair_list,
    pair_count,
    w_query,
    w_key,
    w_value,
    w_out,
    w_orb,
    target,
):
    walkers, rows = elec_pos.shape[1], elec_pos.shape[2]
    count, walks = lax.axis_size("elec"), lax.axis_size("walk")
    width, orbitals = w_query.shape[0], w_orb.shape[2]
    row_local = walkers * rows
    smem = pl.BlockSpec(memory_space=pltpu.SMEM)
    sem = pltpu.SemaphoreType.DMA
    hbm = pl.BlockSpec(memory_space=pltpu.HBM)
    pairs = count // 2
    plain, coded = layout(2 * width // count, width // count, orbitals // LANES)
    chunks = len(plain)
    height = sum(plain[-1])
    long = sum(coded[-1])
    one, many = sem((chunks,)), sem((chunks, pairs - 1))
    depth = rows // BLOCK * NEAR * SLOT
    codes = pl.pallas_call(
        lambda *refs: step_kernel(count, walks, *refs),
        out_shape=jax.ShapeDtypeStruct((2, pairs, long, LANES), I16),
        in_specs=[smem] * 3 + [hbm] * 11,
        out_specs=hbm,
        scratch_shapes=[
            VM((count, ATOM_DEV, width), F32),
            VM((count, 3, ATOM_DEV), F32),
            VM((count, 3, walkers, rows), F32),
            VM((count, 1, rows), jnp.int32),
            VM((2, width), F32),
            VM((width, width), BF16),
            VM((width, width), BF16),
            VM((width, width), BF16),
            VM((width, width), BF16),
            VM((2 * width, orbitals), BF16),
            VM((row_local, orbitals), BF16),
            sem((count - 1, 4)),
            sem((count - 1, 4)),
            sem((11,)),
            VM((3, 8, depth), F32),
            VM((3, depth, width), F32),
            VM((3, rows, rows), F32),
            VM((walkers, rows // BLOCK, BLOCK, width), BF16),
            VM((walkers, 3 * rows // BLOCK, BLOCK, width), BF16),
            VM((walkers, 3 * rows // BLOCK, width, 2 * BLOCK), BF16),
            VM((row_local, width), BF16),
            VM((walkers, rows, width), F32),
            VM((2, pairs, height, LANES), F32),
            VM((2, pairs, long, LANES), I16),
            VM((pairs, height, LANES), F32),
            VM((pairs - 1, long, LANES), I16),
            VM((pairs - 1, long, LANES), I16),
            VM((height, LANES), F32),
            VM((long, LANES), I16),
            VM((long, LANES), I16),
            VM((long, LANES), I16),
        ]
        + [one] * 2
        + [many] * 2
        + [one] * 6
        + [many] * 2
        + [one] * 2
        + [sem((2 * chunks,))],
        compiler_params=pltpu.CompilerParams(
            collective_id=0, has_side_effects=True, vmem_limit_bytes=VMEM_MIB * 1024 * 1024
        ),
        name="whole_step",
    )(
        near_atoms.T,
        pair_list.T,
        pair_count.reshape(1, -1),
        atom_emb,
        atom_pos.T,
        elec_pos,
        spin.reshape(1, rows),
        spin_emb,
        w_query,
        w_key,
        w_value,
        w_out,
        w_orb.reshape(2 * width, orbitals),
        target.reshape(row_local, orbitals),
    )
    piece, tail = 2 * width // count, width // count
    grad_orb, grad_out, loss = pl.pallas_call(
        lambda *refs: plain_kernel(plain, coded, *refs),
        out_shape=(
            jax.ShapeDtypeStruct((2 * width, orbitals), F32),
            jax.ShapeDtypeStruct((width, width), F32),
            jax.ShapeDtypeStruct((1,), F32),
        ),
        in_specs=[hbm],
        out_specs=(hbm, hbm, smem),
        scratch_shapes=[
            VM((2, pairs, long, LANES), I16),
            VM((2 * width, orbitals), F32),
            VM((width, width), F32),
            sem((2 * count + 1,)),
        ],
        compiler_params=pltpu.CompilerParams(vmem_limit_bytes=VMEM_MIB * 1024 * 1024),
        name="decode",
    )(codes)
    return (grad_orb.reshape(2, width, orbitals), grad_out, loss)


def solution(mesh):
    in_specs = (
        P(None, ("parts", "walk"), "elec"),
        P(("parts", "elec"), None),
        P(("parts", "elec"), None),
        P(),
        P(("parts", "elec")),
        P("parts", None),
        P("parts", None),
        P("parts"),
        P(),
        P(),
        P(),
        P(),
        P(),
        P(("parts", "walk"), "elec", None),
    )
    out_specs = (P("parts", None, None), P("parts", None), P("parts"))
    return jax.shard_map(local, mesh=mesh, in_specs=in_specs, out_specs=out_specs, check_vma=False)
```

```python
import math

import jax
import jax.numpy as jnp
from jax import lax
from jax.experimental import pallas as pl
from jax.experimental.pallas import tpu as pltpu
from jax.sharding import PartitionSpec as P

HEADS = 16
BLOCK = 64
ATOM_DEV = 25
NEAR = 2
KMAX = 4
SLOT = 32
LANES = 128
WIDE = 256
TILE = 16
FULL = 32700.0
FINE = 64.0
HOP_US = 2.0
CORE_US = 1.0
CHUNK_US = 0.4
VMEM_MIB = 30
F32 = jnp.float32
BF16 = jnp.bfloat16
I16 = jnp.int16
VM = pltpu.VMEM
NT = (((1,), (1,)), ((), ()))


def encode(x):
    top = jnp.maximum(jnp.max(jnp.abs(x), axis=0, keepdims=True), 1e-30)
    level = jnp.ceil(jnp.log(top) * (FINE / math.log(2.0)))
    scale = jnp.exp2(level * (-1.0 / FINE)) * FULL
    return jnp.round(x * scale).astype(jnp.int32).astype(I16), level


def unit(level):
    return jnp.exp2(level * (1.0 / FINE)) * (1.0 / FULL)


def widen(codes):
    return codes.astype(jnp.int32).astype(F32)


def layout(piece, tail, blocks):
    plain, coded = [], []
    for c in range(blocks):
        plain.append((c * piece, piece, 0))
        coded.append((c * (piece + TILE), piece + TILE))
    plain.append((blocks * piece, 2 * tail, TILE))
    coded.append((blocks * (piece + TILE), 2 * tail + 2 * TILE))
    return plain, coded


def make_steps(pairs, walks, plain, coded, part, out, r1, s2, r2, a2, sz, r3, r4, *sems):
    send_core, recv_core, send_y, recv_y, send_z, recv_z, send_c, recv_c, send_b, recv_b = sems[:10]
    send_y2, recv_y2, send_core2, recv_core2 = sems[10:14]
    chunks = len(plain)
    elec = lax.axis_index("elec")
    wk = lax.axis_index("walk")
    core, y = lax.rem(elec, 2), elec // 2
    mesh_id = pl.DeviceIdType.MESH
    middle = walks // 2
    on_left = wk < middle
    level = jnp.where(on_left, wk, walks - 1 - wk)
    toward = jnp.where(on_left, 1, walks - 1)
    partner = {"elec": y * 2 + 1 - core}
    inward = {"walk": lax.rem(wk + toward, walks)}
    outward = {"walk": lax.rem(wk + walks - toward, walks)}
    inner_level = middle - 1

    def over_y(k):
        return {"elec": lax.rem(y + 1 + k, pairs) * 2 + core}

    def route(src, dst, ssem, rsem, peer):
        return pltpu.make_async_remote_copy(
            src_ref=src,
            dst_ref=dst,
            send_sem=ssem,
            recv_sem=rsem,
            device_id=peer,
            device_id_type=mesh_id,
        )

    def copies(c):
        low, size, extra = plain[c]
        rng = pl.ds(low, size + extra)
        code = pl.ds(*coded[c])
        whole = out.at[core, :, code]
        mine = out.at[core, y, code]
        return dict(
            core=route(
                part.at[1 - core, :, rng], r1.at[:, rng], send_core.at[c], recv_core.at[c], partner
            ),
            y=[
                route(s2.at[k, code], r2.at[k, code], send_y.at[c, k], recv_y.at[c, k], over_y(k))
                for k in range(pairs - 1)
            ],
            z=route(sz.at[code], r3.at[code], send_z.at[c], recv_z.at[c], inward),
            c=route(sz.at[code], r4.at[code], send_c.at[c], recv_c.at[c], inward),
            b=route(mine, mine, send_b.at[c], recv_b.at[c], outward),
            y2=[
                route(mine, mine, send_y2.at[c, k], recv_y2.at[c, k], over_y(k))
                for k in range(pairs - 1)
            ],
            core2=route(whole, whole, send_core2.at[c], recv_core2.at[c], partner),
        )

    flights = [copies(c) for c in range(chunks)]

    def spans(c):
        low, size, extra = plain[c]
        start = coded[c][0]
        groups = [(pl.ds(low, size), pl.ds(start, size))]
        if extra:
            groups.append((pl.ds(low + size, extra), pl.ds(start + size, extra)))
        return groups, pl.ds(start + size + extra, TILE)

    def code_into(c, read, dst):
        groups, scales = spans(c)
        row = lax.broadcasted_iota(jnp.int32, (TILE, LANES), 0)
        marks = None
        for g, (rows, codes) in enumerate(groups):
            body, mark = encode(read(rows))
            dst[codes] = body
            mark = jnp.broadcast_to(mark, (TILE, LANES))
            marks = mark if marks is None else jnp.where(row < TILE // 2, marks, mark)
        dst[scales] = marks.astype(jnp.int32).astype(I16)

    def decoded(c, src):
        groups, scales = spans(c)
        marks = widen(src[scales])
        return [
            (rows, widen(src[codes]) * unit(marks[g * (TILE // 2) : g * (TILE // 2) + 1]))
            for g, (rows, codes) in enumerate(groups)
        ]

    def send_inward(c, key):
        code_into(c, lambda rows: a2[rows], sz)
        flights[c][key].start()

    def pair_done(c):
        flight = flights[c]
        low, size, extra = plain[c]
        rng = pl.ds(low, size + extra)
        flight["core"].wait_recv()
        for k in range(pairs - 1):
            other = lax.rem(y + 1 + k, pairs)
            code_into(c, lambda rows: r1[other, rows] + part[core, other, rows], s2.at[k])
            flight["y"][k].start()
        a2[rng] = r1[y, rng] + part[core, y, rng]

    def step(stage, c):
        flight = flights[c]
        if stage == 0:
            for k, copy in enumerate(flight["y"]):
                copy.wait_recv()
                for rows, value in decoded(c, r2.at[k]):
                    a2[rows] = a2[rows] + value

            if inner_level > 0:

                @pl.when(level == 0)
                def _():
                    send_inward(c, "z")

        elif stage < middle:

            @pl.when(level == stage)
            def _():
                flight["z"].wait_recv()
                for rows, value in decoded(c, r3):
                    a2[rows] = a2[rows] + value
                if stage < inner_level:
                    send_inward(c, "z")

        if stage == inner_level:

            @pl.when(level == inner_level)
            def _():
                send_inward(c, "c")

        back = stage - middle
        if back == 0:

            @pl.when(level == inner_level)
            def _():
                own = decoded(c, sz)
                flight["c"].wait_recv()
                for (rows, value), (_, other) in zip(own, decoded(c, r4)):
                    a2[rows] = value + other
                code_into(c, lambda rows: a2[rows], out.at[core, y])
                if inner_level > 0:
                    flight["b"].start()
                for copy in flight["y2"]:
                    copy.start()
        elif 0 < back < middle:

            @pl.when(level == inner_level - back)
            def _():
                flight["b"].wait_recv()
                if back < inner_level:
                    flight["b"].start()
                for copy in flight["y2"]:
                    copy.start()

        if back == middle:
            for copy in flight["y2"]:
                copy.wait_recv()
            flight["core2"].start()
        elif back == middle + 1:
            flight["core2"].wait_recv()

    def begin(c):
        flights[c]["core"].start()

    stages = 2 * middle + 2

    def after(done):
        events = [(t, -1, c) for c, t in enumerate(done)]
        ready = list(done)
        for stage in range(stages):
            wait = CORE_US if stage == stages - 1 else HOP_US
            before = -1e9
            for c in range(chunks):
                before = max(ready[c] + wait, before + CHUNK_US)
                ready[c] = before
                events.append((before, stage, c))
        return sorted(events)

    def drain():
        for flight in flights:
            for copy in [flight["core"], flight["core2"]] + flight["y"] + flight["y2"]:
                copy.wait_send()

            @pl.when(level < inner_level)
            def _():
                flight["z"].wait_send()

            @pl.when(level == inner_level)
            def _():
                flight["c"].wait_send()

            @pl.when(level > 0)
            def _():
                flight["b"].wait_send()

    return begin, pair_done, step, after, drain


def thirds(x):
    rest = x - x.astype(BF16).astype(F32)
    return x, rest, rest - rest.astype(BF16).astype(F32)


def step_kernel(
    count,
    walks,
    near,
    pairs,
    pair_n,
    emb,
    pos,
    epos,
    spin,
    *rest,
):
    outer, result, inner = rest[:7], rest[7], rest[8:]
    gemb, gpos, gep, gsp = inner[:4]
    held = inner[4:11]
    spin_emb, w_query, w_key, w_value, w_out, w_orb, target = held
    send, recv, local_sem = inner[11:14]
    pstack, estack, e_s, q_s, v_s, kt_s, h_s, att_s, part = inner[14:23]
    me = lax.axis_index("elec")
    barrier = pltpu.get_barrier_semaphore()
    for k in range(count - 1):
        pl.semaphore_signal(
            barrier,
            inc=1,
            device_id={"elec": lax.rem(me + 1 + k, count)},
            device_id_type=pl.DeviceIdType.MESH,
        )
    wk = lax.axis_index("walk")

    @pl.when(wk > 0)
    def _():
        pl.semaphore_signal(
            barrier,
            inc=1,
            device_id={"walk": lax.rem(wk + walks - 1, walks)},
            device_id_type=pl.DeviceIdType.MESH,
        )

    @pl.when(wk < walks - 1)
    def _():
        pl.semaphore_signal(
            barrier,
            inc=1,
            device_id={"walk": lax.rem(wk + 1, walks)},
            device_id_type=pl.DeviceIdType.MESH,
        )

    ends = jnp.where(wk > 0, 1, 0) + jnp.where(wk < walks - 1, 1, 0)
    small = ((emb, gemb), (pos, gpos), (epos, gep), (spin, gsp))
    own = [
        pltpu.make_async_copy(src, dst.at[me], local_sem.at[i])
        for i, (src, dst) in enumerate(small)
    ]
    loads = [
        pltpu.make_async_copy(src, dst, local_sem.at[4 + i])
        for i, (src, dst) in enumerate(zip(outer, held))
    ]
    for copy in own + loads:
        copy.start()
    pl.semaphore_wait(barrier, count - 1 + ends)
    copies = []
    for k in range(count - 1):
        for i, (src, dst) in enumerate(small):
            copy = pltpu.make_async_remote_copy(
                src_ref=src,
                dst_ref=dst.at[me],
                send_sem=send.at[k, i],
                recv_sem=recv.at[k, i],
                device_id={"elec": lax.rem(me + 1 + k, count)},
                device_id_type=pl.DeviceIdType.MESH,
            )
            copy.start()
            copies.append(copy)
    walkers, rows = gep.shape[2], gep.shape[3]
    width = w_query.shape[0]
    head = width // HEADS
    per_device = rows // BLOCK
    owners = (me, lax.rem(me + count - 1, count), lax.rem(me + 1, count))
    pstack[...] = jnp.zeros_like(pstack)
    estack[...] = jnp.zeros_like(estack)
    e_s[...] = jnp.zeros_like(e_s)
    first_half = lax.broadcasted_iota(jnp.int32, (width, 2 * BLOCK), 1) < BLOCK
    depth = NEAR * SLOT
    lane_id = lax.broadcasted_iota(jnp.int32, (BLOCK, 2 * depth), 1)
    low_lanes = lax.broadcasted_iota(jnp.int32, (walkers * BLOCK, 2 * depth), 1) < depth
    places, valid = [], []
    for p in range(per_device):
        query_block = me * per_device + p
        for slot in range(KMAX):
            used = slot < pair_n[0, query_block]
            key_block = jnp.where(used, pairs[slot, query_block], query_block)
            away = lax.rem(key_block // per_device - me + count, count)
            side = jnp.where(away == 0, 0, jnp.where(away == 1, 2, 1))
            places.append(side * per_device + lax.rem(key_block, per_device))
            valid.append(jnp.where(used, 1.0, 0.0).astype(F32))
    for copy in own + loads[:4]:
        copy.wait()
    wk_t = w_key[...].astype(F32).T.astype(BF16)
    for copy in copies:
        copy.wait_recv()
    spin_cols = []
    for j, owner in enumerate(owners):
        for p in range(per_device):
            for n in range(NEAR):
                group = near[n, owner * per_device + p]
                for low in (n * SLOT, depth + n * SLOT):
                    pstack[j, p, 0:3, low : low + ATOM_DEV] = gpos[group]
                estack[j, p, n * SLOT : n * SLOT + ATOM_DEV, :] = gemb[group]
            estack[j, p, ATOM_DEV : ATOM_DEV + 2, :] = spin_emb[...]
        electron = gep[owner]
        for axis in range(3):
            e_s[j, axis * walkers : (axis + 1) * walkers, :] = electron[axis]
        e_s[j, 3 * walkers : 3 * walkers + 1, :] = gsp[owner].astype(F32)
        columns = e_s[j].T
        up_one = columns[:, 3 * walkers : 3 * walkers + 1]
        spin_cols.append(up_one)
        blocks = []
        for p in range(per_device):
            pieces = []
            mine = slice(p * BLOCK, (p + 1) * BLOCK)
            up = up_one[mine]
            for w in range(walkers):
                distance = jnp.zeros((BLOCK, 2 * depth), F32)
                for axis in range(3):
                    at = axis * walkers + w
                    spacing = columns[mine, at : at + 1] - pstack[j, p, axis : axis + 1, :]
                    distance = distance + spacing * spacing
                close = 1.0 / (1.0 + distance)
                close = jnp.where(lane_id % depth == ATOM_DEV, 1.0 - up, close)
                close = jnp.where(lane_id % depth == ATOM_DEV + 1, up, close)
                pieces.append(close)
            one, two, three = thirds(jnp.concatenate(pieces, axis=0))
            high = jnp.where(low_lanes, one, two).astype(BF16)
            rest = jnp.where(low_lanes, one, three).astype(BF16)
            e_one, e_two, e_three = [part.astype(BF16) for part in thirds(estack[j, p])]
            blocks.append(
                jnp.dot(
                    jnp.concatenate([high, high, rest], axis=1),
                    jnp.concatenate([e_one, e_one, e_two, e_two, e_three, e_one], axis=0),
                    preferred_element_type=F32,
                ).astype(BF16)
            )
        hidden = jnp.concatenate(blocks, axis=0)
        values = jnp.dot(hidden, w_value[...], preferred_element_type=F32).astype(BF16)
        keys_t = lax.dot_general(wk_t, hidden, NT, preferred_element_type=F32)
        for p in range(per_device):
            at = j * per_device + p
            for w in range(walkers):
                start = (p * walkers + w) * BLOCK
                v_s[w, at] = values[start : start + BLOCK]
            for w in range(0, walkers, 2):
                start = (p * walkers + w) * BLOCK
                across = keys_t[:, start : start + 2 * BLOCK]
                turned = jnp.concatenate([across[:, BLOCK:], across[:, :BLOCK]], axis=1)
                kt_s[w, at] = jnp.where(first_half, across, turned).astype(BF16)
                kt_s[w + 1, at] = jnp.where(first_half, turned, across).astype(BF16)
        if j == 0:
            queries = jnp.dot(hidden, w_query[...], preferred_element_type=F32).astype(BF16)
            queries = (queries.astype(F32) * (1.0 / math.sqrt(head))).astype(BF16)
            for w in range(walkers):
                for p in range(per_device):
                    start = (p * walkers + w) * BLOCK
                    h_s[w, p] = hidden[start : start + BLOCK]
                    q_s[w, p] = queries[start : start + BLOCK]
    group = rows // head
    head_lane = lax.broadcasted_iota(jnp.int32, (BLOCK, rows), 1) // head
    head_masks = [jnp.where(head_lane == h, 1.0, 0.0).astype(BF16) for h in range(group)]
    half_row = lax.broadcasted_iota(jnp.int32, (1, 2 * BLOCK), 1) < BLOCK

    def walker(w, carry):
        for p in range(per_device):
            slots = range(p * KMAX, (p + 1) * KMAX)
            values = jnp.concatenate([v_s[w, places[s]] for s in slots], axis=0)
            keys_t = jnp.concatenate(
                [
                    jnp.where(first_half, kt_s[w, places[s]], kt_s[w, places[s + 1]])
                    for s in slots[::2]
                ],
                axis=1,
            )
            allowed = jnp.concatenate(
                [jnp.where(half_row, valid[s], valid[s + 1]) for s in slots[::2]], axis=1
            )
            for low in range(0, width, rows):
                query = q_s[w, p, :, low : low + rows]
                spread = jnp.concatenate([query * mask for mask in head_masks], axis=0)
                scores = jnp.dot(spread, keys_t[low : low + rows], preferred_element_type=F32)
                top = jnp.max(scores, axis=1, keepdims=True)
                weights = jnp.exp(scores - top) * allowed
                total = jnp.sum(weights, axis=1, keepdims=True)
                mixed = jnp.dot(
                    weights.astype(BF16), values[:, low : low + rows], preferred_element_type=F32
                )
                above, below = mixed[:BLOCK], jnp.broadcast_to(total[:BLOCK], (BLOCK, rows))
                for h in range(1, group):
                    mine = slice(h * BLOCK, (h + 1) * BLOCK)
                    above = jnp.where(head_lane == h, mixed[mine], above)
                    below = jnp.where(head_lane == h, total[mine], below)
                att_s[w, p * BLOCK : (p + 1) * BLOCK, low : low + rows] = above / below
        return carry

    lax.fori_loop(0, walkers, walker, 0)
    for copy in loads[4:]:
        copy.wait()
    attended_wide = jnp.concatenate([att_s[w] for w in range(walkers)], axis=0)
    attended = attended_wide.astype(BF16)
    mixed_out = jnp.dot(attended, w_out[...], preferred_element_type=F32)
    hidden = h_s[...].reshape(walkers * rows, width).astype(F32)
    hidden_out = (hidden + mixed_out).astype(BF16).astype(F32)
    spin_row = gsp[me].astype(F32)
    spin_col = spin_cols[0]
    up_col = jnp.concatenate([spin_col] * walkers, axis=0) > 0.5
    up_lane = jnp.concatenate([spin_row] * walkers, axis=1) > 0.5
    split = jnp.concatenate(
        [jnp.where(up_col, 0.0, hidden_out), jnp.where(up_col, hidden_out, 0.0)], axis=1
    ).astype(BF16)
    hidden_t = hidden_out.T
    split_t = jnp.concatenate(
        [jnp.where(up_lane, 0.0, hidden_t), jnp.where(up_lane, hidden_t, 0.0)], axis=0
    ).astype(BF16)
    orbitals = target.shape[1]
    both_rows = 2 * width
    pairs = count // 2
    piece = both_rows // count
    tail = width // count
    blocks = orbitals // LANES
    plain, coded = layout(piece, tail, blocks)
    begin, pair_done, step, after, drain = make_steps(
        pairs, walks, plain, coded, part, result, *inner[23:]
    )
    share = 1.0 / (walkers * rows * count * lax.axis_size("walk"))
    backward = None
    loss = jnp.zeros((1, WIDE), F32)
    halves = WIDE // LANES
    for c in range(orbitals // WIDE):
        columns = slice(c * WIDE, (c + 1) * WIDE)
        w_piece = w_orb[:, columns]
        residual = jnp.dot(split, w_piece, preferred_element_type=F32) - target[
            :, columns
        ].astype(F32)
        loss = loss + jnp.sum(residual * residual, axis=0, keepdims=True)
        signal = residual.astype(BF16)
        grad = share * jnp.dot(split_t, signal, preferred_element_type=F32)
        for h in range(halves):
            low = plain[halves * c + h][0]
            for q in range(count):
                part[q // pairs, q % pairs, low : low + piece, :] = grad[
                    q * piece : (q + 1) * piece, h * LANES : (h + 1) * LANES
                ]
            begin(halves * c + h)
        if c > 0:
            for h in range(halves):
                pair_done(halves * (c - 1) + h)
        term = lax.dot_general(signal, w_piece, NT, preferred_element_type=F32)
        backward = term if backward is None else backward + term
    chosen = jnp.where(up_col, backward[:, width:], backward[:, :width]).astype(BF16)
    att_t = attended_wide.T.astype(BF16)
    grad = share * jnp.dot(att_t, chosen, preferred_element_type=F32)
    spread = (0.5 * share) * jnp.sum(loss, axis=1, keepdims=True)
    base = plain[-1][0]
    for q in range(count):
        here = part.at[q // pairs, q % pairs]
        for h in range(halves):
            here[base + h * tail : base + (h + 1) * tail, :] = grad[
                q * tail : (q + 1) * tail, h * LANES : (h + 1) * LANES
            ]
        here[base + halves * tail : base + halves * tail + TILE, :] = jnp.broadcast_to(
            spread, (TILE, LANES)
        )
    begin(blocks)
    early = blocks - halves
    done = [(c // halves) * 0.7 - 2.0 if c < early else 0.3 * (c - early) for c in range(blocks + 1)]
    for _, stage, c in after(done):
        if stage >= 0:
            step(stage, c)
        elif c >= early:
            pair_done(c)
    drain()
    for copy in copies:
        copy.wait_send()


def plain_kernel(plain, coded, codes, g_orb, g_out, g_loss, orb, low, sems):
    pairs = codes.shape[1]
    count = 2 * pairs
    piece, tail = orb.shape[0] // count, low.shape[0] // count
    copies = []
    def emit(src, dst):
        copy = pltpu.make_async_copy(src, dst, sems.at[len(copies)])
        copy.start()
        copies.append(copy)

    for q in range(count):
        here = codes.at[q // pairs, q % pairs]
        rows = slice(q * piece, (q + 1) * piece)
        for c, ((_, size, extra), (start, length)) in enumerate(zip(plain, coded)):
            marks = widen(here[start + size + extra : start + length])
            value = widen(here[start : start + size]) * unit(marks[:1])
            if not extra:
                orb[rows, c * LANES : (c + 1) * LANES] = value
                continue
            for h in range(low.shape[1] // LANES):
                low[q * tail : (q + 1) * tail, h * LANES : (h + 1) * LANES] = value[
                    h * tail : (h + 1) * tail
                ]
        emit(orb.at[rows], g_orb.at[rows])
        if q == 0:
            mark = marks[TILE // 2 : TILE // 2 + 1]
            sums = widen(here[start + size : start + size + extra]) * unit(mark)
            g_loss[0] = jnp.max(sums)
    emit(low, g_out)
    for copy in copies:
        copy.wait()


def pinned(*arrays):
    return [pltpu.with_memory_space_constraint(array, pltpu.HBM) for array in arrays]


def local(
    elec_pos,
    atom_pos,
    atom_emb,
    spin_emb,
    spin,
    near_atoms,
    pair_list,
    pair_count,
    w_query,
    w_key,
    w_value,
    w_out,
    w_orb,
    target,
):
    walkers, rows = elec_pos.shape[1], elec_pos.shape[2]
    count, walks = lax.axis_size("elec"), lax.axis_size("walk")
    width, orbitals = w_query.shape[0], w_orb.shape[2]
    row_local = walkers * rows
    smem = pl.BlockSpec(memory_space=pltpu.SMEM)
    sem = pltpu.SemaphoreType.DMA
    hbm = pl.BlockSpec(memory_space=pltpu.HBM)
    pairs = count // 2
    plain, coded = layout(2 * width // count, width // count, orbitals // LANES)
    chunks = len(plain)
    height = sum(plain[-1])
    long = sum(coded[-1])
    one, many = sem((chunks,)), sem((chunks, pairs - 1))
    depth = NEAR * SLOT
    codes = pl.pallas_call(
        lambda *refs: step_kernel(count, walks, *refs),
        out_shape=VM((2, pairs, long, LANES), I16),
        in_specs=[smem] * 3 + [hbm] * 11,
        out_specs=pl.BlockSpec(memory_space=VM),
        scratch_shapes=[
            VM((count, ATOM_DEV, width), F32),
            VM((count, 3, ATOM_DEV), F32),
            VM((count, 3, walkers, rows), F32),
            VM((count, 1, rows), jnp.int32),
            VM((2, width), F32),
            VM((width, width), BF16),
            VM((width, width), BF16),
            VM((width, width), BF16),
            VM((width, width), BF16),
            VM((2 * width, orbitals), BF16),
            VM((row_local, orbitals), BF16),
            sem((count - 1, 4)),
            sem((count - 1, 4)),
            sem((11,)),
            VM((3, rows // BLOCK, 8, 2 * depth), F32),
            VM((3, rows // BLOCK, depth, width), F32),
            VM((3, rows, rows), F32),
            VM((walkers, rows // BLOCK, BLOCK, width), BF16),
            VM((walkers, 3 * rows // BLOCK, BLOCK, width), BF16),
            VM((walkers, 3 * rows // BLOCK, width, 2 * BLOCK), BF16),
            VM((walkers, rows // BLOCK, BLOCK, width), BF16),
            VM((walkers, rows, width), F32),
            VM((2, pairs, height, LANES), F32),
            VM((pairs, height, LANES), F32),
            VM((pairs - 1, long, LANES), I16),
            VM((pairs - 1, long, LANES), I16),
            VM((height, LANES), F32),
            VM((long, LANES), I16),
            VM((long, LANES), I16),
            VM((long, LANES), I16),
        ]
        + [one] * 2
        + [many] * 2
        + [one] * 6
        + [many] * 2
        + [one] * 2,
        compiler_params=pltpu.CompilerParams(
            collective_id=0, has_side_effects=True, vmem_limit_bytes=VMEM_MIB * 1024 * 1024
        ),
        name="whole_step",
    )(
        *pinned(
        near_atoms.T,
        pair_list.T,
        pair_count.reshape(1, -1),
        atom_emb,
        atom_pos.T,
        elec_pos,
        spin.reshape(1, rows),
        spin_emb,
        w_query,
        w_key,
        w_value,
        w_out,
        w_orb.reshape(2 * width, orbitals),
        target.reshape(row_local, orbitals),
        )
    )
    piece, tail = 2 * width // count, width // count
    grad_orb, grad_out, loss = pl.pallas_call(
        lambda *refs: plain_kernel(plain, coded, *refs),
        out_shape=(
            jax.ShapeDtypeStruct((2 * width, orbitals), F32),
            jax.ShapeDtypeStruct((width, width), F32),
            jax.ShapeDtypeStruct((1,), F32),
        ),
        in_specs=[pl.BlockSpec(memory_space=VM)],
        out_specs=(hbm, hbm, smem),
        scratch_shapes=[
            VM((2 * width, orbitals), F32),
            VM((width, width), F32),
            sem((count + 1,)),
        ],
        compiler_params=pltpu.CompilerParams(vmem_limit_bytes=VMEM_MIB * 1024 * 1024),
        name="decode",
    )(codes)
    return (grad_orb.reshape(2, width, orbitals), grad_out, loss)


def solution(mesh):
    in_specs = (
        P(None, ("parts", "walk"), "elec"),
        P(("parts", "elec"), None),
        P(("parts", "elec"), None),
        P(),
        P(("parts", "elec")),
        P("parts", None),
        P("parts", None),
        P("parts"),
        P(),
        P(),
        P(),
        P(),
        P(),
        P(("parts", "walk"), "elec", None),
    )
    out_specs = (P("parts", None, None), P("parts", None), P("parts"))
    return jax.shard_map(local, mesh=mesh, in_specs=in_specs, out_specs=out_specs, check_vma=False)
```

```python
import math

import jax
import jax.numpy as jnp
from jax import lax
from jax.experimental import pallas as pl
from jax.experimental.pallas import tpu as pltpu
from jax.sharding import PartitionSpec as P

HEADS = 16
BLOCK = 64
ATOM_DEV = 25
NEAR = 2
KMAX = 4
SLOT = 32
LANES = 128
WIDE = 256
TILE = 16
FULL = 32700.0
FINE = 64.0
HOP_US = 2.0
CORE_US = 1.0
CHUNK_US = 0.4
VMEM_MIB = 30
F32 = jnp.float32
BF16 = jnp.bfloat16
I16 = jnp.int16
VM = pltpu.VMEM
NT = (((1,), (1,)), ((), ()))


def encode(x):
    top = jnp.maximum(jnp.max(jnp.abs(x), axis=0, keepdims=True), 1e-30)
    level = jnp.ceil(jnp.log(top) * (FINE / math.log(2.0)))
    scale = jnp.exp2(level * (-1.0 / FINE)) * FULL
    return jnp.round(x * scale).astype(jnp.int32).astype(I16), level


def unit(level):
    return jnp.exp2(level * (1.0 / FINE)) * (1.0 / FULL)


def widen(codes):
    return codes.astype(jnp.int32).astype(F32)


def layout(piece, tail, blocks):
    plain, coded = [], []
    for c in range(blocks):
        plain.append((c * piece, piece, 0))
        coded.append((c * (piece + TILE), piece + TILE))
    plain.append((blocks * piece, 2 * tail, TILE))
    coded.append((blocks * (piece + TILE), 2 * tail + 2 * TILE))
    return plain, coded


def make_steps(pairs, walks, plain, coded, part, out, r1, s2, r2, a2, sz, r3, r4, *sems):
    send_core, recv_core, send_y, recv_y, send_z, recv_z, send_c, recv_c, send_b, recv_b = sems[:10]
    send_y2, recv_y2, send_core2, recv_core2 = sems[10:14]
    chunks = len(plain)
    elec = lax.axis_index("elec")
    wk = lax.axis_index("walk")
    core, y = lax.rem(elec, 2), elec // 2
    mesh_id = pl.DeviceIdType.MESH
    middle = walks // 2
    on_left = wk < middle
    level = jnp.where(on_left, wk, walks - 1 - wk)
    toward = jnp.where(on_left, 1, walks - 1)
    partner = {"elec": y * 2 + 1 - core}
    inward = {"walk": lax.rem(wk + toward, walks)}
    outward = {"walk": lax.rem(wk + walks - toward, walks)}
    inner_level = middle - 1

    def over_y(k):
        return {"elec": lax.rem(y + 1 + k, pairs) * 2 + core}

    def route(src, dst, ssem, rsem, peer):
        return pltpu.make_async_remote_copy(
            src_ref=src,
            dst_ref=dst,
            send_sem=ssem,
            recv_sem=rsem,
            device_id=peer,
            device_id_type=mesh_id,
        )

    def copies(c):
        low, size, extra = plain[c]
        rng = pl.ds(low, size + extra)
        code = pl.ds(*coded[c])
        whole = out.at[core, :, code]
        mine = out.at[core, y, code]
        return dict(
            core=route(
                part.at[1 - core, :, rng], r1.at[:, rng], send_core.at[c], recv_core.at[c], partner
            ),
            y=[
                route(s2.at[k, code], r2.at[k, code], send_y.at[c, k], recv_y.at[c, k], over_y(k))
                for k in range(pairs - 1)
            ],
            z=route(sz.at[code], r3.at[code], send_z.at[c], recv_z.at[c], inward),
            c=route(sz.at[code], r4.at[code], send_c.at[c], recv_c.at[c], inward),
            b=route(mine, mine, send_b.at[c], recv_b.at[c], outward),
            y2=[
                route(mine, mine, send_y2.at[c, k], recv_y2.at[c, k], over_y(k))
                for k in range(pairs - 1)
            ],
            core2=route(whole, whole, send_core2.at[c], recv_core2.at[c], partner),
        )

    flights = [copies(c) for c in range(chunks)]

    def spans(c):
        low, size, extra = plain[c]
        start = coded[c][0]
        groups = [(pl.ds(low, size), pl.ds(start, size))]
        if extra:
            groups.append((pl.ds(low + size, extra), pl.ds(start + size, extra)))
        return groups, pl.ds(start + size + extra, TILE)

    def code_into(c, read, dst):
        groups, scales = spans(c)
        row = lax.broadcasted_iota(jnp.int32, (TILE, LANES), 0)
        marks = None
        for g, (rows, codes) in enumerate(groups):
            body, mark = encode(read(rows))
            dst[codes] = body
            mark = jnp.broadcast_to(mark, (TILE, LANES))
            marks = mark if marks is None else jnp.where(row < TILE // 2, marks, mark)
        dst[scales] = marks.astype(jnp.int32).astype(I16)

    def decoded(c, src):
        groups, scales = spans(c)
        marks = widen(src[scales])
        return [
            (rows, widen(src[codes]) * unit(marks[g * (TILE // 2) : g * (TILE // 2) + 1]))
            for g, (rows, codes) in enumerate(groups)
        ]

    def send_inward(c, key):
        code_into(c, lambda rows: a2[rows], sz)
        flights[c][key].start()

    def pair_done(c):
        flight = flights[c]
        low, size, extra = plain[c]
        rng = pl.ds(low, size + extra)
        flight["core"].wait_recv()
        for k in range(pairs - 1):
            other = lax.rem(y + 1 + k, pairs)
            code_into(c, lambda rows: r1[other, rows] + part[core, other, rows], s2.at[k])
            flight["y"][k].start()
        a2[rng] = r1[y, rng] + part[core, y, rng]

    def step(stage, c):
        flight = flights[c]
        if stage == 0:
            for k, copy in enumerate(flight["y"]):
                copy.wait_recv()
                for rows, value in decoded(c, r2.at[k]):
                    a2[rows] = a2[rows] + value

            if inner_level > 0:

                @pl.when(level == 0)
                def _():
                    send_inward(c, "z")

        elif stage < middle:

            @pl.when(level == stage)
            def _():
                flight["z"].wait_recv()
                for rows, value in decoded(c, r3):
                    a2[rows] = a2[rows] + value
                if stage < inner_level:
                    send_inward(c, "z")

        if stage == inner_level:

            @pl.when(level == inner_level)
            def _():
                send_inward(c, "c")

        back = stage - middle
        if back == 0:

            @pl.when(level == inner_level)
            def _():
                own = decoded(c, sz)
                flight["c"].wait_recv()
                for (rows, value), (_, other) in zip(own, decoded(c, r4)):
                    a2[rows] = value + other
                code_into(c, lambda rows: a2[rows], out.at[core, y])
                if inner_level > 0:
                    flight["b"].start()
                for copy in flight["y2"]:
                    copy.start()
        elif 0 < back < middle:

            @pl.when(level == inner_level - back)
            def _():
                flight["b"].wait_recv()
                if back < inner_level:
                    flight["b"].start()
                for copy in flight["y2"]:
                    copy.start()

        if back == middle:
            for copy in flight["y2"]:
                copy.wait_recv()
            flight["core2"].start()
        elif back == middle + 1:
            flight["core2"].wait_recv()

    def begin(c):
        flights[c]["core"].start()

    stages = 2 * middle + 2

    def after(done):
        events = [(t, -1, c) for c, t in enumerate(done)]
        ready = list(done)
        for stage in range(stages):
            wait = CORE_US if stage == stages - 1 else HOP_US
            before = -1e9
            for c in range(chunks):
                before = max(ready[c] + wait, before + CHUNK_US)
                ready[c] = before
                events.append((before, stage, c))
        return sorted(events)

    def drain():
        for flight in flights:
            for copy in [flight["core"], flight["core2"]] + flight["y"] + flight["y2"]:
                copy.wait_send()

            @pl.when(level < inner_level)
            def _():
                flight["z"].wait_send()

            @pl.when(level == inner_level)
            def _():
                flight["c"].wait_send()

            @pl.when(level > 0)
            def _():
                flight["b"].wait_send()

    return begin, pair_done, step, after, drain


def thirds(x):
    rest = x - x.astype(BF16).astype(F32)
    return x, rest, rest - rest.astype(BF16).astype(F32)


def step_kernel(
    count,
    walks,
    near_ref,
    pairs_ref,
    pair_n_ref,
    emb,
    pos,
    epos,
    spin,
    *rest,
):
    outer, result, inner = rest[:7], rest[7], rest[8:-4]
    near, pairs, pair_n, table_sem = rest[-4:]
    gemb, gpos, gep, gsp = inner[:4]
    held = inner[4:11]
    spin_emb, w_query, w_key, w_value, w_out, w_orb, target = held
    send, recv, local_sem = inner[11:14]
    pstack, estack, e_s, q_s, v_s, kt_s, h_s, att_s, part = inner[14:23]
    me = lax.axis_index("elec")
    barrier = pltpu.get_barrier_semaphore()
    for k in range(count - 1):
        pl.semaphore_signal(
            barrier,
            inc=1,
            device_id={"elec": lax.rem(me + 1 + k, count)},
            device_id_type=pl.DeviceIdType.MESH,
        )
    wk = lax.axis_index("walk")

    @pl.when(wk > 0)
    def _():
        pl.semaphore_signal(
            barrier,
            inc=1,
            device_id={"walk": lax.rem(wk + walks - 1, walks)},
            device_id_type=pl.DeviceIdType.MESH,
        )

    @pl.when(wk < walks - 1)
    def _():
        pl.semaphore_signal(
            barrier,
            inc=1,
            device_id={"walk": lax.rem(wk + 1, walks)},
            device_id_type=pl.DeviceIdType.MESH,
        )

    ends = jnp.where(wk > 0, 1, 0) + jnp.where(wk < walks - 1, 1, 0)
    small = ((emb, gemb), (pos, gpos), (epos, gep), (spin, gsp))
    own = [
        pltpu.make_async_copy(src, dst.at[me], local_sem.at[i])
        for i, (src, dst) in enumerate(small)
    ]
    loads = [
        pltpu.make_async_copy(src, dst, local_sem.at[4 + i])
        for i, (src, dst) in enumerate(zip(outer, held))
    ]
    tables = [
        pltpu.make_async_copy(src, dst, table_sem.at[i])
        for i, (src, dst) in enumerate(
            ((near_ref, near), (pairs_ref, pairs), (pair_n_ref, pair_n))
        )
    ]
    for copy in own + tables + loads:
        copy.start()
    for copy in own:
        copy.wait()
    pl.semaphore_wait(barrier, count - 1 + ends)
    copies = []
    for k in range(count - 1):
        for i, (_, dst) in enumerate(small):
            copy = pltpu.make_async_remote_copy(
                src_ref=dst.at[me],
                dst_ref=dst.at[me],
                send_sem=send.at[k, i],
                recv_sem=recv.at[k, i],
                device_id={"elec": lax.rem(me + 1 + k, count)},
                device_id_type=pl.DeviceIdType.MESH,
            )
            copy.start()
            copies.append(copy)
    walkers, rows = gep.shape[2], gep.shape[3]
    width = w_query.shape[0]
    head = width // HEADS
    per_device = rows // BLOCK
    owners = (me, lax.rem(me + count - 1, count), lax.rem(me + 1, count))
    pstack[...] = jnp.zeros_like(pstack)
    estack[...] = jnp.zeros_like(estack)
    e_s[...] = jnp.zeros_like(e_s)
    first_half = lax.broadcasted_iota(jnp.int32, (width, 2 * BLOCK), 1) < BLOCK
    depth = NEAR * SLOT
    lane_id = lax.broadcasted_iota(jnp.int32, (BLOCK, 2 * depth), 1)
    low_lanes = lax.broadcasted_iota(jnp.int32, (walkers * BLOCK, 2 * depth), 1) < depth
    for copy in tables:
        copy.wait()
    places, valid = [], []
    for p in range(per_device):
        query_block = me * per_device + p
        for slot in range(KMAX):
            used = slot < pair_n[0, query_block]
            key_block = jnp.where(used, pairs[slot, query_block], query_block)
            away = lax.rem(key_block // per_device - me + count, count)
            side = jnp.where(away == 0, 0, jnp.where(away == 1, 2, 1))
            places.append(side * per_device + lax.rem(key_block, per_device))
            valid.append(jnp.where(used, 1.0, 0.0).astype(F32))
    for copy in loads[:4]:
        copy.wait()
    wk_t = w_key[...].astype(F32).T.astype(BF16)
    for copy in copies:
        copy.wait_recv()
    spin_cols = []
    for j, owner in enumerate(owners):
        for p in range(per_device):
            for n in range(NEAR):
                group = near[n, owner * per_device + p]
                for low in (n * SLOT, depth + n * SLOT):
                    pstack[j, p, 0:3, low : low + ATOM_DEV] = gpos[group]
                estack[j, p, n * SLOT : n * SLOT + ATOM_DEV, :] = gemb[group]
            estack[j, p, ATOM_DEV : ATOM_DEV + 2, :] = spin_emb[...]
        electron = gep[owner]
        for axis in range(3):
            e_s[j, axis * walkers : (axis + 1) * walkers, :] = electron[axis]
        e_s[j, 3 * walkers : 3 * walkers + 1, :] = gsp[owner].astype(F32)
        columns = e_s[j].T
        up_one = columns[:, 3 * walkers : 3 * walkers + 1]
        spin_cols.append(up_one)
        blocks = []
        for p in range(per_device):
            pieces = []
            mine = slice(p * BLOCK, (p + 1) * BLOCK)
            up = up_one[mine]
            for w in range(walkers):
                distance = jnp.zeros((BLOCK, 2 * depth), F32)
                for axis in range(3):
                    at = axis * walkers + w
                    spacing = columns[mine, at : at + 1] - pstack[j, p, axis : axis + 1, :]
                    distance = distance + spacing * spacing
                close = 1.0 / (1.0 + distance)
                close = jnp.where(lane_id % depth == ATOM_DEV, 1.0 - up, close)
                close = jnp.where(lane_id % depth == ATOM_DEV + 1, up, close)
                pieces.append(close)
            one, two, three = thirds(jnp.concatenate(pieces, axis=0))
            high = jnp.where(low_lanes, one, two).astype(BF16)
            rest = jnp.where(low_lanes, one, three).astype(BF16)
            e_one, e_two, e_three = [part.astype(BF16) for part in thirds(estack[j, p])]
            blocks.append(
                jnp.dot(
                    jnp.concatenate([high, high, rest], axis=1),
                    jnp.concatenate([e_one, e_one, e_two, e_two, e_three, e_one], axis=0),
                    preferred_element_type=F32,
                ).astype(BF16)
            )
        hidden = jnp.concatenate(blocks, axis=0)
        values = jnp.dot(hidden, w_value[...], preferred_element_type=F32).astype(BF16)
        keys_t = lax.dot_general(wk_t, hidden, NT, preferred_element_type=F32)
        for p in range(per_device):
            at = j * per_device + p
            for w in range(walkers):
                start = (p * walkers + w) * BLOCK
                v_s[w, at] = values[start : start + BLOCK]
            for w in range(0, walkers, 2):
                start = (p * walkers + w) * BLOCK
                across = keys_t[:, start : start + 2 * BLOCK]
                turned = jnp.concatenate([across[:, BLOCK:], across[:, :BLOCK]], axis=1)
                kt_s[w, at] = jnp.where(first_half, across, turned).astype(BF16)
                kt_s[w + 1, at] = jnp.where(first_half, turned, across).astype(BF16)
        if j == 0:
            queries = jnp.dot(hidden, w_query[...], preferred_element_type=F32).astype(BF16)
            queries = (queries.astype(F32) * (1.0 / math.sqrt(head))).astype(BF16)
            for w in range(walkers):
                for p in range(per_device):
                    start = (p * walkers + w) * BLOCK
                    h_s[w, p] = hidden[start : start + BLOCK]
                    q_s[w, p] = queries[start : start + BLOCK]
    group = rows // head
    head_lane = lax.broadcasted_iota(jnp.int32, (BLOCK, rows), 1) // head
    head_masks = [jnp.where(head_lane == h, 1.0, 0.0).astype(BF16) for h in range(group)]
    half_row = lax.broadcasted_iota(jnp.int32, (1, 2 * BLOCK), 1) < BLOCK

    def walker(w):
        for p in range(per_device):
            slots = range(p * KMAX, (p + 1) * KMAX)
            values = jnp.concatenate([v_s[w, places[s]] for s in slots], axis=0)
            keys_t = jnp.concatenate(
                [
                    jnp.where(first_half, kt_s[w, places[s]], kt_s[w, places[s + 1]])
                    for s in slots[::2]
                ],
                axis=1,
            )
            allowed = jnp.concatenate(
                [jnp.where(half_row, valid[s], valid[s + 1]) for s in slots[::2]], axis=1
            )
            for low in range(0, width, rows):
                query = q_s[w, p, :, low : low + rows]
                spread = jnp.concatenate([query * mask for mask in head_masks], axis=0)
                scores = jnp.dot(spread, keys_t[low : low + rows], preferred_element_type=F32)
                top = jnp.max(scores, axis=1, keepdims=True)
                weights = jnp.exp(scores - top) * allowed
                total = jnp.sum(weights, axis=1, keepdims=True)
                mixed = jnp.dot(
                    weights.astype(BF16), values[:, low : low + rows], preferred_element_type=F32
                )
                above, below = mixed[:BLOCK], jnp.broadcast_to(total[:BLOCK], (BLOCK, rows))
                for h in range(1, group):
                    mine = slice(h * BLOCK, (h + 1) * BLOCK)
                    above = jnp.where(head_lane == h, mixed[mine], above)
                    below = jnp.where(head_lane == h, total[mine], below)
                att_s[w, p * BLOCK : (p + 1) * BLOCK, low : low + rows] = above / below

    for w in range(walkers):
        walker(w)
    for copy in loads[4:]:
        copy.wait()
    attended_wide = jnp.concatenate([att_s[w] for w in range(walkers)], axis=0)
    attended = attended_wide.astype(BF16)
    mixed_out = jnp.dot(attended, w_out[...], preferred_element_type=F32)
    hidden = h_s[...].reshape(walkers * rows, width).astype(F32)
    hidden_out = (hidden + mixed_out).astype(BF16).astype(F32)
    spin_row = gsp[me].astype(F32)
    spin_col = spin_cols[0]
    up_col = jnp.concatenate([spin_col] * walkers, axis=0) > 0.5
    up_lane = jnp.concatenate([spin_row] * walkers, axis=1) > 0.5
    split = jnp.concatenate(
        [jnp.where(up_col, 0.0, hidden_out), jnp.where(up_col, hidden_out, 0.0)], axis=1
    ).astype(BF16)
    hidden_t = hidden_out.T
    split_t = jnp.concatenate(
        [jnp.where(up_lane, 0.0, hidden_t), jnp.where(up_lane, hidden_t, 0.0)], axis=0
    ).astype(BF16)
    orbitals = target.shape[1]
    both_rows = 2 * width
    pairs = count // 2
    piece = both_rows // count
    tail = width // count
    blocks = orbitals // LANES
    plain, coded = layout(piece, tail, blocks)
    begin, pair_done, step, after, drain = make_steps(
        pairs, walks, plain, coded, part, result, *inner[23:]
    )
    share = 1.0 / (walkers * rows * count * lax.axis_size("walk"))
    backward = None
    loss = jnp.zeros((1, WIDE), F32)
    halves = WIDE // LANES
    for c in range(orbitals // WIDE):
        columns = slice(c * WIDE, (c + 1) * WIDE)
        w_piece = w_orb[:, columns]
        residual = jnp.dot(split, w_piece, preferred_element_type=F32) - target[
            :, columns
        ].astype(F32)
        loss = loss + jnp.sum(residual * residual, axis=0, keepdims=True)
        signal = residual.astype(BF16)
        grad = share * jnp.dot(split_t, signal, preferred_element_type=F32)
        for h in range(halves):
            low = plain[halves * c + h][0]
            for q in range(count):
                part[q // pairs, q % pairs, low : low + piece, :] = grad[
                    q * piece : (q + 1) * piece, h * LANES : (h + 1) * LANES
                ]
            begin(halves * c + h)
        if c > 0:
            for h in range(halves):
                pair_done(halves * (c - 1) + h)
        term = lax.dot_general(signal, w_piece, NT, preferred_element_type=F32)
        backward = term if backward is None else backward + term
    chosen = jnp.where(up_col, backward[:, width:], backward[:, :width]).astype(BF16)
    att_t = attended_wide.T.astype(BF16)
    grad = share * jnp.dot(att_t, chosen, preferred_element_type=F32)
    spread = (0.5 * share) * jnp.sum(loss, axis=1, keepdims=True)
    base = plain[-1][0]
    for q in range(count):
        here = part.at[q // pairs, q % pairs]
        for h in range(halves):
            here[base + h * tail : base + (h + 1) * tail, :] = grad[
                q * tail : (q + 1) * tail, h * LANES : (h + 1) * LANES
            ]
        here[base + halves * tail : base + halves * tail + TILE, :] = jnp.broadcast_to(
            spread, (TILE, LANES)
        )
    begin(blocks)
    early = blocks - halves
    done = [(c // halves) * 0.7 - 2.0 if c < early else 0.3 * (c - early) for c in range(blocks + 1)]
    for _, stage, c in after(done):
        if stage >= 0:
            step(stage, c)
        elif c >= early:
            pair_done(c)
    drain()
    for copy in copies:
        copy.wait_send()


def plain_kernel(plain, coded, codes, g_orb, g_out, g_loss, orb, low, sems):
    pairs = codes.shape[1]
    count = 2 * pairs
    piece, tail = orb.shape[0] // count, low.shape[0] // count
    copies = []
    def emit(src, dst):
        copy = pltpu.make_async_copy(src, dst, sems.at[len(copies)])
        copy.start()
        copies.append(copy)

    for q in range(count):
        here = codes.at[q // pairs, q % pairs]
        rows = slice(q * piece, (q + 1) * piece)
        for c, ((_, size, extra), (start, length)) in enumerate(zip(plain, coded)):
            marks = widen(here[start + size + extra : start + length])
            value = widen(here[start : start + size]) * unit(marks[:1])
            if not extra:
                orb[rows, c * LANES : (c + 1) * LANES] = value
                continue
            for h in range(low.shape[1] // LANES):
                low[q * tail : (q + 1) * tail, h * LANES : (h + 1) * LANES] = value[
                    h * tail : (h + 1) * tail
                ]
        emit(orb.at[rows], g_orb.at[rows])
        if q == 0:
            mark = marks[TILE // 2 : TILE // 2 + 1]
            sums = widen(here[start + size : start + size + extra]) * unit(mark)
            g_loss[0] = jnp.max(sums)
    emit(low, g_out)
    for copy in copies:
        copy.wait()


def pinned(*arrays):
    return [pltpu.with_memory_space_constraint(array, pltpu.HBM) for array in arrays]


def local(
    elec_pos,
    atom_pos,
    atom_emb,
    spin_emb,
    spin,
    near_atoms,
    pair_list,
    pair_count,
    w_query,
    w_key,
    w_value,
    w_out,
    w_orb,
    target,
):
    walkers, rows = elec_pos.shape[1], elec_pos.shape[2]
    count, walks = lax.axis_size("elec"), lax.axis_size("walk")
    width, orbitals = w_query.shape[0], w_orb.shape[2]
    row_local = walkers * rows
    smem = pl.BlockSpec(memory_space=pltpu.SMEM)
    sem = pltpu.SemaphoreType.DMA
    hbm = pl.BlockSpec(memory_space=pltpu.HBM)
    pairs = count // 2
    plain, coded = layout(2 * width // count, width // count, orbitals // LANES)
    chunks = len(plain)
    height = sum(plain[-1])
    long = sum(coded[-1])
    one, many = sem((chunks,)), sem((chunks, pairs - 1))
    depth = NEAR * SLOT
    lists = (near_atoms.T, pair_list.T, pair_count.reshape(1, -1))
    codes = pl.pallas_call(
        lambda *refs: step_kernel(count, walks, *refs),
        out_shape=VM((2, pairs, long, LANES), I16),
        in_specs=[hbm] * 14,
        out_specs=pl.BlockSpec(memory_space=VM),
        scratch_shapes=[
            VM((count, ATOM_DEV, width), F32),
            VM((count, 3, ATOM_DEV), F32),
            VM((count, 3, walkers, rows), F32),
            VM((count, 1, rows), jnp.int32),
            VM((2, width), F32),
            VM((width, width), BF16),
            VM((width, width), BF16),
            VM((width, width), BF16),
            VM((width, width), BF16),
            VM((2 * width, orbitals), BF16),
            VM((row_local, orbitals), BF16),
            sem((count - 1, 4)),
            sem((count - 1, 4)),
            sem((11,)),
            VM((3, rows // BLOCK, 8, 2 * depth), F32),
            VM((3, rows // BLOCK, depth, width), F32),
            VM((3, rows, rows), F32),
            VM((walkers, rows // BLOCK, BLOCK, width), BF16),
            VM((walkers, 3 * rows // BLOCK, BLOCK, width), BF16),
            VM((walkers, 3 * rows // BLOCK, width, 2 * BLOCK), BF16),
            VM((walkers, rows // BLOCK, BLOCK, width), BF16),
            VM((walkers, rows, width), F32),
            VM((2, pairs, height, LANES), F32),
            VM((pairs, height, LANES), F32),
            VM((pairs - 1, long, LANES), I16),
            VM((pairs - 1, long, LANES), I16),
            VM((height, LANES), F32),
            VM((long, LANES), I16),
            VM((long, LANES), I16),
            VM((long, LANES), I16),
        ]
        + [one] * 2
        + [many] * 2
        + [one] * 6
        + [many] * 2
        + [one] * 2
        + [pltpu.SMEM(table.shape, jnp.int32) for table in lists]
        + [sem((3,))],
        compiler_params=pltpu.CompilerParams(
            collective_id=0, has_side_effects=True, vmem_limit_bytes=VMEM_MIB * 1024 * 1024
        ),
        name="whole_step",
    )(
        *pinned(
        *lists,
        atom_emb,
        atom_pos.T,
        elec_pos,
        spin.reshape(1, rows),
        spin_emb,
        w_query,
        w_key,
        w_value,
        w_out,
        w_orb.reshape(2 * width, orbitals),
        target.reshape(row_local, orbitals),
        )
    )
    piece, tail = 2 * width // count, width // count
    grad_orb, grad_out, loss = pl.pallas_call(
        lambda *refs: plain_kernel(plain, coded, *refs),
        out_shape=(
            jax.ShapeDtypeStruct((2 * width, orbitals), F32),
            jax.ShapeDtypeStruct((width, width), F32),
            jax.ShapeDtypeStruct((1,), F32),
        ),
        in_specs=[pl.BlockSpec(memory_space=VM)],
        out_specs=(hbm, hbm, smem),
        scratch_shapes=[
            VM((2 * width, orbitals), F32),
            VM((width, width), F32),
            sem((count + 1,)),
        ],
        compiler_params=pltpu.CompilerParams(vmem_limit_bytes=VMEM_MIB * 1024 * 1024),
        name="decode",
    )(codes)
    return (grad_orb.reshape(2, width, orbitals), grad_out, loss)


def solution(mesh):
    in_specs = (
        P(None, ("parts", "walk"), "elec"),
        P(("parts", "elec"), None),
        P(("parts", "elec"), None),
        P(),
        P(("parts", "elec")),
        P("parts", None),
        P("parts", None),
        P("parts"),
        P(),
        P(),
        P(),
        P(),
        P(),
        P(("parts", "walk"), "elec", None),
    )
    out_specs = (P("parts", None, None), P("parts", None), P("parts"))
    return jax.shard_map(local, mesh=mesh, in_specs=in_specs, out_specs=out_specs, check_vma=False)
```

```python
import math

import jax
import jax.numpy as jnp
from jax import lax
from jax.experimental import pallas as pl
from jax.experimental.pallas import tpu as pltpu
from jax.sharding import PartitionSpec as P

HEADS = 16
BLOCK = 64
ATOM_DEV = 25
NEAR = 2
KMAX = 4
SLOT = 32
LANES = 128
WIDE = 256
TILE = 16
FULL = 32700.0
FINE = 64.0
HOP_US = 2.0
CORE_US = 1.0
CHUNK_US = 0.5
VMEM_MIB = 30
F32 = jnp.float32
BF16 = jnp.bfloat16
I16 = jnp.int16
VM = pltpu.VMEM
NT = (((1,), (1,)), ((), ()))


def encode(x):
    top = jnp.maximum(jnp.max(jnp.abs(x), axis=0, keepdims=True), 1e-30)
    level = jnp.ceil(jnp.log(top) * (FINE / math.log(2.0)))
    scale = jnp.exp2(level * (-1.0 / FINE)) * FULL
    return jnp.round(x * scale).astype(jnp.int32).astype(I16), level


def unit(level):
    return jnp.exp2(level * (1.0 / FINE)) * (1.0 / FULL)


def widen(codes):
    return codes.astype(jnp.int32).astype(F32)


def layout(piece, tail, blocks):
    plain, coded = [], []
    for c in range(blocks):
        plain.append((c * piece, piece, 0))
        coded.append((c * (piece + TILE), piece + TILE))
    plain.append((blocks * piece, 2 * tail, TILE))
    coded.append((blocks * (piece + TILE), 2 * tail + 2 * TILE))
    return plain, coded


def make_steps(pairs, walks, plain, coded, part, out, r1, s2, r2, a2, sz, r3, r4, *sems):
    send_core, recv_core, send_y, recv_y, send_z, recv_z, send_c, recv_c, send_b, recv_b = sems[:10]
    send_y2, recv_y2, send_core2, recv_core2 = sems[10:14]
    chunks = len(plain)
    elec = lax.axis_index("elec")
    wk = lax.axis_index("walk")
    core, y = lax.rem(elec, 2), elec // 2
    mesh_id = pl.DeviceIdType.MESH
    middle = walks // 2
    on_left = wk < middle
    level = jnp.where(on_left, wk, walks - 1 - wk)
    toward = jnp.where(on_left, 1, walks - 1)
    partner = {"elec": y * 2 + 1 - core}
    inward = {"walk": lax.rem(wk + toward, walks)}
    outward = {"walk": lax.rem(wk + walks - toward, walks)}
    inner_level = middle - 1

    def over_y(k):
        return {"elec": lax.rem(y + 1 + k, pairs) * 2 + core}

    def route(src, dst, ssem, rsem, peer):
        return pltpu.make_async_remote_copy(
            src_ref=src,
            dst_ref=dst,
            send_sem=ssem,
            recv_sem=rsem,
            device_id=peer,
            device_id_type=mesh_id,
        )

    def copies(c):
        low, size, extra = plain[c]
        rng = pl.ds(low, size + extra)
        code = pl.ds(*coded[c])
        whole = out.at[core, :, code]
        mine = out.at[core, y, code]
        return dict(
            core=route(
                part.at[1 - core, :, rng], r1.at[:, rng], send_core.at[c], recv_core.at[c], partner
            ),
            y=[
                route(s2.at[k, code], r2.at[k, code], send_y.at[c, k], recv_y.at[c, k], over_y(k))
                for k in range(pairs - 1)
            ],
            z=route(sz.at[code], r3.at[code], send_z.at[c], recv_z.at[c], inward),
            c=route(sz.at[code], r4.at[code], send_c.at[c], recv_c.at[c], inward),
            b=route(mine, mine, send_b.at[c], recv_b.at[c], outward),
            y2=[
                route(mine, mine, send_y2.at[c, k], recv_y2.at[c, k], over_y(k))
                for k in range(pairs - 1)
            ],
            core2=route(whole, whole, send_core2.at[c], recv_core2.at[c], partner),
        )

    flights = [copies(c) for c in range(chunks)]

    def spans(c):
        low, size, extra = plain[c]
        start = coded[c][0]
        groups = [(pl.ds(low, size), pl.ds(start, size))]
        if extra:
            groups.append((pl.ds(low + size, extra), pl.ds(start + size, extra)))
        return groups, pl.ds(start + size + extra, TILE)

    def code_into(c, read, dst):
        groups, scales = spans(c)
        row = lax.broadcasted_iota(jnp.int32, (TILE, LANES), 0)
        marks = None
        for g, (rows, codes) in enumerate(groups):
            body, mark = encode(read(rows))
            dst[codes] = body
            mark = jnp.broadcast_to(mark, (TILE, LANES))
            marks = mark if marks is None else jnp.where(row < TILE // 2, marks, mark)
        dst[scales] = marks.astype(jnp.int32).astype(I16)

    def decoded(c, src):
        groups, scales = spans(c)
        marks = widen(src[scales])
        return [
            (rows, widen(src[codes]) * unit(marks[g * (TILE // 2) : g * (TILE // 2) + 1]))
            for g, (rows, codes) in enumerate(groups)
        ]

    def send_inward(c, key):
        code_into(c, lambda rows: a2[rows], sz)
        flights[c][key].start()

    def pair_done(c):
        flight = flights[c]
        low, size, extra = plain[c]
        rng = pl.ds(low, size + extra)
        flight["core"].wait_recv()
        for k in range(pairs - 1):
            other = lax.rem(y + 1 + k, pairs)
            code_into(c, lambda rows: r1[other, rows] + part[core, other, rows], s2.at[k])
            flight["y"][k].start()
        a2[rng] = r1[y, rng] + part[core, y, rng]

    def step(stage, c):
        flight = flights[c]
        if stage == 0:
            for k, copy in enumerate(flight["y"]):
                copy.wait_recv()
                for rows, value in decoded(c, r2.at[k]):
                    a2[rows] = a2[rows] + value

            if inner_level > 0:

                @pl.when(level == 0)
                def _():
                    send_inward(c, "z")

        elif stage < middle:

            @pl.when(level == stage)
            def _():
                flight["z"].wait_recv()
                for rows, value in decoded(c, r3):
                    a2[rows] = a2[rows] + value
                if stage < inner_level:
                    send_inward(c, "z")

        if stage == inner_level:

            @pl.when(level == inner_level)
            def _():
                send_inward(c, "c")

        back = stage - middle
        if back == 0:

            @pl.when(level == inner_level)
            def _():
                own = decoded(c, sz)
                flight["c"].wait_recv()
                for (rows, value), (_, other) in zip(own, decoded(c, r4)):
                    a2[rows] = value + other
                code_into(c, lambda rows: a2[rows], out.at[core, y])
                if inner_level > 0:
                    flight["b"].start()
                for copy in flight["y2"]:
                    copy.start()
        elif 0 < back < middle:

            @pl.when(level == inner_level - back)
            def _():
                flight["b"].wait_recv()
                if back < inner_level:
                    flight["b"].start()
                for copy in flight["y2"]:
                    copy.start()

        if back == middle:
            for copy in flight["y2"]:
                copy.wait_recv()
            flight["core2"].start()
        elif back == middle + 1:
            flight["core2"].wait_recv()

    def begin(c):
        flights[c]["core"].start()

    stages = 2 * middle + 2

    def after(done):
        events = [(t, -1, c) for c, t in enumerate(done)]
        ready = list(done)
        for stage in range(stages):
            wait = CORE_US if stage == stages - 1 else HOP_US
            before = -1e9
            for c in range(chunks):
                before = max(ready[c] + wait, before + CHUNK_US)
                ready[c] = before
                events.append((before, stage, c))
        return sorted(events)

    def drain():
        for flight in flights:
            for copy in [flight["core"], flight["core2"]] + flight["y"] + flight["y2"]:
                copy.wait_send()

            @pl.when(level < inner_level)
            def _():
                flight["z"].wait_send()

            @pl.when(level == inner_level)
            def _():
                flight["c"].wait_send()

            @pl.when(level > 0)
            def _():
                flight["b"].wait_send()

    return begin, pair_done, step, after, drain


def thirds(x):
    rest = x - x.astype(BF16).astype(F32)
    return x, rest, rest - rest.astype(BF16).astype(F32)


def step_kernel(
    count,
    walks,
    near_ref,
    pairs_ref,
    pair_n_ref,
    emb,
    pos,
    epos,
    spin,
    *rest,
):
    outer, result, inner = rest[:7], rest[7], rest[8:-4]
    near, pairs, pair_n, table_sem = rest[-4:]
    gemb, gpos, gep, gsp = inner[:4]
    held = inner[4:11]
    spin_emb, w_query, w_key, w_value, w_out, w_orb, target = held
    send, recv, local_sem = inner[11:14]
    pstack, estack, e_s, q_s, v_s, kt_s, h_s, att_s, part = inner[14:23]
    me = lax.axis_index("elec")
    barrier = pltpu.get_barrier_semaphore()
    for k in range(count - 1):
        pl.semaphore_signal(
            barrier,
            inc=1,
            device_id={"elec": lax.rem(me + 1 + k, count)},
            device_id_type=pl.DeviceIdType.MESH,
        )
    wk = lax.axis_index("walk")

    @pl.when(wk > 0)
    def _():
        pl.semaphore_signal(
            barrier,
            inc=1,
            device_id={"walk": lax.rem(wk + walks - 1, walks)},
            device_id_type=pl.DeviceIdType.MESH,
        )

    @pl.when(wk < walks - 1)
    def _():
        pl.semaphore_signal(
            barrier,
            inc=1,
            device_id={"walk": lax.rem(wk + 1, walks)},
            device_id_type=pl.DeviceIdType.MESH,
        )

    ends = jnp.where(wk > 0, 1, 0) + jnp.where(wk < walks - 1, 1, 0)
    small = ((emb, gemb), (pos, gpos), (epos, gep), (spin, gsp))
    own = [
        pltpu.make_async_copy(src, dst.at[me], local_sem.at[i])
        for i, (src, dst) in enumerate(small)
    ]
    loads = [
        pltpu.make_async_copy(src, dst, local_sem.at[4 + i])
        for i, (src, dst) in enumerate(zip(outer, held))
    ]
    tables = [
        pltpu.make_async_copy(src, dst, table_sem.at[i])
        for i, (src, dst) in enumerate(
            ((near_ref, near), (pairs_ref, pairs), (pair_n_ref, pair_n))
        )
    ]
    for copy in own + tables + loads:
        copy.start()
    for copy in own:
        copy.wait()
    pl.semaphore_wait(barrier, count - 1 + ends)
    copies = []
    for k in range(count - 1):
        for i, (_, dst) in enumerate(small):
            copy = pltpu.make_async_remote_copy(
                src_ref=dst.at[me],
                dst_ref=dst.at[me],
                send_sem=send.at[k, i],
                recv_sem=recv.at[k, i],
                device_id={"elec": lax.rem(me + 1 + k, count)},
                device_id_type=pl.DeviceIdType.MESH,
            )
            copy.start()
            copies.append(copy)
    walkers, rows = gep.shape[2], gep.shape[3]
    width = w_query.shape[0]
    head = width // HEADS
    per_device = rows // BLOCK
    owners = (me, lax.rem(me + count - 1, count), lax.rem(me + 1, count))
    pstack[...] = jnp.zeros_like(pstack)
    estack[...] = jnp.zeros_like(estack)
    e_s[...] = jnp.zeros_like(e_s)
    first_half = lax.broadcasted_iota(jnp.int32, (width, 2 * BLOCK), 1) < BLOCK
    depth = NEAR * SLOT
    lane_id = lax.broadcasted_iota(jnp.int32, (BLOCK, 2 * depth), 1)
    low_lanes = lax.broadcasted_iota(jnp.int32, (walkers * BLOCK, 2 * depth), 1) < depth
    for copy in tables:
        copy.wait()
    places, valid = [], []
    for p in range(per_device):
        query_block = me * per_device + p
        for slot in range(KMAX):
            used = slot < pair_n[0, query_block]
            key_block = jnp.where(used, pairs[slot, query_block], query_block)
            away = lax.rem(key_block // per_device - me + count, count)
            side = jnp.where(away == 0, 0, jnp.where(away == 1, 2, 1))
            places.append(side * per_device + lax.rem(key_block, per_device))
            valid.append(jnp.where(used, 1.0, 0.0).astype(F32))
    for copy in loads[:4]:
        copy.wait()
    wk_t = w_key[...].astype(F32).T.astype(BF16)
    for copy in copies:
        copy.wait_recv()
    spin_cols = []
    for j, owner in enumerate(owners):
        for p in range(per_device):
            for n in range(NEAR):
                group = near[n, owner * per_device + p]
                for low in (n * SLOT, depth + n * SLOT):
                    pstack[j, p, 0:3, low : low + ATOM_DEV] = gpos[group]
                estack[j, p, n * SLOT : n * SLOT + ATOM_DEV, :] = gemb[group]
            estack[j, p, ATOM_DEV : ATOM_DEV + 2, :] = spin_emb[...]
        electron = gep[owner]
        for axis in range(3):
            e_s[j, axis * walkers : (axis + 1) * walkers, :] = electron[axis]
        e_s[j, 3 * walkers : 3 * walkers + 1, :] = gsp[owner].astype(F32)
        columns = e_s[j].T
        up_one = columns[:, 3 * walkers : 3 * walkers + 1]
        spin_cols.append(up_one)
        blocks = []
        for p in range(per_device):
            pieces = []
            mine = slice(p * BLOCK, (p + 1) * BLOCK)
            up = up_one[mine]
            for w in range(walkers):
                distance = jnp.zeros((BLOCK, 2 * depth), F32)
                for axis in range(3):
                    at = axis * walkers + w
                    spacing = columns[mine, at : at + 1] - pstack[j, p, axis : axis + 1, :]
                    distance = distance + spacing * spacing
                close = 1.0 / (1.0 + distance)
                close = jnp.where(lane_id % depth == ATOM_DEV, 1.0 - up, close)
                close = jnp.where(lane_id % depth == ATOM_DEV + 1, up, close)
                pieces.append(close)
            one, two, three = thirds(jnp.concatenate(pieces, axis=0))
            high = jnp.where(low_lanes, one, two).astype(BF16)
            rest = jnp.where(low_lanes, one, three).astype(BF16)
            e_one, e_two, e_three = [part.astype(BF16) for part in thirds(estack[j, p])]
            blocks.append(
                jnp.dot(
                    jnp.concatenate([high, high, rest], axis=1),
                    jnp.concatenate([e_one, e_one, e_two, e_two, e_three, e_one], axis=0),
                    preferred_element_type=F32,
                ).astype(BF16)
            )
        hidden = jnp.concatenate(blocks, axis=0)
        values = jnp.dot(hidden, w_value[...], preferred_element_type=F32).astype(BF16)
        keys_t = lax.dot_general(wk_t, hidden, NT, preferred_element_type=F32)
        for p in range(per_device):
            at = j * per_device + p
            for w in range(walkers):
                start = (p * walkers + w) * BLOCK
                v_s[w, at] = values[start : start + BLOCK]
            for w in range(0, walkers, 2):
                start = (p * walkers + w) * BLOCK
                across = keys_t[:, start : start + 2 * BLOCK]
                turned = jnp.concatenate([across[:, BLOCK:], across[:, :BLOCK]], axis=1)
                kt_s[w, at] = jnp.where(first_half, across, turned).astype(BF16)
                kt_s[w + 1, at] = jnp.where(first_half, turned, across).astype(BF16)
        if j == 0:
            queries = jnp.dot(hidden, w_query[...], preferred_element_type=F32).astype(BF16)
            queries = (queries.astype(F32) * (1.0 / math.sqrt(head))).astype(BF16)
            for w in range(walkers):
                for p in range(per_device):
                    start = (p * walkers + w) * BLOCK
                    h_s[w, p] = hidden[start : start + BLOCK]
                    q_s[w, p] = queries[start : start + BLOCK]
    group = rows // head
    head_lane = lax.broadcasted_iota(jnp.int32, (BLOCK, rows), 1) // head
    head_masks = [jnp.where(head_lane == h, 1.0, 0.0).astype(BF16) for h in range(group)]
    half_row = lax.broadcasted_iota(jnp.int32, (1, 2 * BLOCK), 1) < BLOCK

    def listed(w, p):
        slots = range(p * KMAX, (p + 1) * KMAX)
        values = jnp.concatenate([v_s[w, places[s]] for s in slots], axis=0)
        keys_t = jnp.concatenate(
            [
                jnp.where(first_half, kt_s[w, places[s]], kt_s[w, places[s + 1]])
                for s in slots[::2]
            ],
            axis=1,
        )
        allowed = jnp.concatenate(
            [jnp.where(half_row, valid[s], valid[s + 1]) for s in slots[::2]], axis=1
        )
        return values, keys_t, allowed

    def score(w, p, low, keys_t):
        query = q_s[w, p, :, low : low + rows]
        spread = jnp.concatenate([query * mask for mask in head_masks], axis=0)
        return jnp.dot(spread, keys_t[low : low + rows], preferred_element_type=F32)

    def attend(w, p, low, scores, values, allowed):
        top = jnp.max(scores, axis=1, keepdims=True)
        weights = jnp.exp(scores - top) * allowed
        total = jnp.sum(weights, axis=1, keepdims=True)
        mixed = jnp.dot(
            weights.astype(BF16), values[:, low : low + rows], preferred_element_type=F32
        )
        above, below = mixed[:BLOCK], jnp.broadcast_to(total[:BLOCK], (BLOCK, rows))
        for h in range(1, group):
            mine = slice(h * BLOCK, (h + 1) * BLOCK)
            above = jnp.where(head_lane == h, mixed[mine], above)
            below = jnp.where(head_lane == h, total[mine], below)
        att_s[w, p * BLOCK : (p + 1) * BLOCK, low : low + rows] = above / below

    waiting = None
    for w in range(walkers):
        for p in range(per_device):
            values, keys_t, allowed = listed(w, p)
            for low in range(0, width, rows):
                scores = score(w, p, low, keys_t)
                if waiting is not None:
                    attend(*waiting)
                waiting = (w, p, low, scores, values, allowed)
    attend(*waiting)
    for copy in loads[4:]:
        copy.wait()
    attended_wide = jnp.concatenate([att_s[w] for w in range(walkers)], axis=0)
    attended = attended_wide.astype(BF16)
    mixed_out = jnp.dot(attended, w_out[...], preferred_element_type=F32)
    hidden = h_s[...].reshape(walkers * rows, width).astype(F32)
    hidden_out = (hidden + mixed_out).astype(BF16).astype(F32)
    spin_row = gsp[me].astype(F32)
    spin_col = spin_cols[0]
    up_col = jnp.concatenate([spin_col] * walkers, axis=0) > 0.5
    up_lane = jnp.concatenate([spin_row] * walkers, axis=1) > 0.5
    split = jnp.concatenate(
        [jnp.where(up_col, 0.0, hidden_out), jnp.where(up_col, hidden_out, 0.0)], axis=1
    ).astype(BF16)
    hidden_t = hidden_out.T
    split_t = jnp.concatenate(
        [jnp.where(up_lane, 0.0, hidden_t), jnp.where(up_lane, hidden_t, 0.0)], axis=0
    ).astype(BF16)
    orbitals = target.shape[1]
    both_rows = 2 * width
    pairs = count // 2
    piece = both_rows // count
    tail = width // count
    blocks = orbitals // LANES
    plain, coded = layout(piece, tail, blocks)
    begin, pair_done, step, after, drain = make_steps(
        pairs, walks, plain, coded, part, result, *inner[23:]
    )
    share = 1.0 / (walkers * rows * count * lax.axis_size("walk"))
    backward = None
    loss = jnp.zeros((1, WIDE), F32)
    halves = WIDE // LANES
    for c in range(orbitals // WIDE):
        columns = slice(c * WIDE, (c + 1) * WIDE)
        w_piece = w_orb[:, columns]
        residual = jnp.dot(split, w_piece, preferred_element_type=F32) - target[
            :, columns
        ].astype(F32)
        loss = loss + jnp.sum(residual * residual, axis=0, keepdims=True)
        signal = residual.astype(BF16)
        grad = share * jnp.dot(split_t, signal, preferred_element_type=F32)
        for h in range(halves):
            low = plain[halves * c + h][0]
            for q in range(count):
                part[q // pairs, q % pairs, low : low + piece, :] = grad[
                    q * piece : (q + 1) * piece, h * LANES : (h + 1) * LANES
                ]
            begin(halves * c + h)
        if c > 0:
            for h in range(halves):
                pair_done(halves * (c - 1) + h)
        term = lax.dot_general(signal, w_piece, NT, preferred_element_type=F32)
        backward = term if backward is None else backward + term
    chosen = jnp.where(up_col, backward[:, width:], backward[:, :width]).astype(BF16)
    att_t = attended_wide.T.astype(BF16)
    grad = share * jnp.dot(att_t, chosen, preferred_element_type=F32)
    spread = (0.5 * share) * jnp.sum(loss, axis=1, keepdims=True)
    base = plain[-1][0]
    for q in range(count):
        here = part.at[q // pairs, q % pairs]
        for h in range(halves):
            here[base + h * tail : base + (h + 1) * tail, :] = grad[
                q * tail : (q + 1) * tail, h * LANES : (h + 1) * LANES
            ]
        here[base + halves * tail : base + halves * tail + TILE, :] = jnp.broadcast_to(
            spread, (TILE, LANES)
        )
    begin(blocks)
    early = blocks - halves
    done = [(c // halves) * 0.7 - 2.0 if c < early else 0.3 * (c - early) for c in range(blocks + 1)]
    for _, stage, c in after(done):
        if stage >= 0:
            step(stage, c)
        elif c >= early:
            pair_done(c)
    drain()
    for copy in copies:
        copy.wait_send()


def plain_kernel(plain, coded, codes, g_orb, g_out, g_loss, orb, low, sems):
    pairs = codes.shape[1]
    count = 2 * pairs
    piece, tail = orb.shape[0] // count, low.shape[0] // count
    copies = []
    def emit(src, dst):
        copy = pltpu.make_async_copy(src, dst, sems.at[len(copies)])
        copy.start()
        copies.append(copy)

    for q in range(count):
        here = codes.at[q // pairs, q % pairs]
        rows = slice(q * piece, (q + 1) * piece)
        for c, ((_, size, extra), (start, length)) in enumerate(zip(plain, coded)):
            marks = widen(here[start + size + extra : start + length])
            value = widen(here[start : start + size]) * unit(marks[:1])
            if not extra:
                orb[rows, c * LANES : (c + 1) * LANES] = value
                continue
            for h in range(low.shape[1] // LANES):
                low[q * tail : (q + 1) * tail, h * LANES : (h + 1) * LANES] = value[
                    h * tail : (h + 1) * tail
                ]
        emit(orb.at[rows], g_orb.at[rows])
        if q == 0:
            mark = marks[TILE // 2 : TILE // 2 + 1]
            sums = widen(here[start + size : start + size + extra]) * unit(mark)
            g_loss[0] = jnp.max(sums)
    emit(low, g_out)
    for copy in copies:
        copy.wait()


def pinned(*arrays):
    return [pltpu.with_memory_space_constraint(array, pltpu.HBM) for array in arrays]


def local(
    elec_pos,
    atom_pos,
    atom_emb,
    spin_emb,
    spin,
    near_atoms,
    pair_list,
    pair_count,
    w_query,
    w_key,
    w_value,
    w_out,
    w_orb,
    target,
):
    walkers, rows = elec_pos.shape[1], elec_pos.shape[2]
    count, walks = lax.axis_size("elec"), lax.axis_size("walk")
    width, orbitals = w_query.shape[0], w_orb.shape[2]
    row_local = walkers * rows
    smem = pl.BlockSpec(memory_space=pltpu.SMEM)
    sem = pltpu.SemaphoreType.DMA
    hbm = pl.BlockSpec(memory_space=pltpu.HBM)
    pairs = count // 2
    plain, coded = layout(2 * width // count, width // count, orbitals // LANES)
    chunks = len(plain)
    height = sum(plain[-1])
    long = sum(coded[-1])
    one, many = sem((chunks,)), sem((chunks, pairs - 1))
    depth = NEAR * SLOT
    lists = (near_atoms.T, pair_list.T, pair_count.reshape(1, -1))
    codes = pl.pallas_call(
        lambda *refs: step_kernel(count, walks, *refs),
        out_shape=VM((2, pairs, long, LANES), I16),
        in_specs=[hbm] * 14,
        out_specs=pl.BlockSpec(memory_space=VM),
        scratch_shapes=[
            VM((count, ATOM_DEV, width), F32),
            VM((count, 3, ATOM_DEV), F32),
            VM((count, 3, walkers, rows), F32),
            VM((count, 1, rows), jnp.int32),
            VM((2, width), F32),
            VM((width, width), BF16),
            VM((width, width), BF16),
            VM((width, width), BF16),
            VM((width, width), BF16),
            VM((2 * width, orbitals), BF16),
            VM((row_local, orbitals), BF16),
            sem((count - 1, 4)),
            sem((count - 1, 4)),
            sem((11,)),
            VM((3, rows // BLOCK, 8, 2 * depth), F32),
            VM((3, rows // BLOCK, depth, width), F32),
            VM((3, rows, rows), F32),
            VM((walkers, rows // BLOCK, BLOCK, width), BF16),
            VM((walkers, 3 * rows // BLOCK, BLOCK, width), BF16),
            VM((walkers, 3 * rows // BLOCK, width, 2 * BLOCK), BF16),
            VM((walkers, rows // BLOCK, BLOCK, width), BF16),
            VM((walkers, rows, width), F32),
            VM((2, pairs, height, LANES), F32),
            VM((pairs, height, LANES), F32),
            VM((pairs - 1, long, LANES), I16),
            VM((pairs - 1, long, LANES), I16),
            VM((height, LANES), F32),
            VM((long, LANES), I16),
            VM((long, LANES), I16),
            VM((long, LANES), I16),
        ]
        + [one] * 2
        + [many] * 2
        + [one] * 6
        + [many] * 2
        + [one] * 2
        + [pltpu.SMEM(table.shape, jnp.int32) for table in lists]
        + [sem((3,))],
        compiler_params=pltpu.CompilerParams(
            collective_id=0, has_side_effects=True, vmem_limit_bytes=VMEM_MIB * 1024 * 1024
        ),
        name="whole_step",
    )(
        *pinned(
        *lists,
        atom_emb,
        atom_pos.T,
        elec_pos,
        spin.reshape(1, rows),
        spin_emb,
        w_query,
        w_key,
        w_value,
        w_out,
        w_orb.reshape(2 * width, orbitals),
        target.reshape(row_local, orbitals),
        )
    )
    piece, tail = 2 * width // count, width // count
    grad_orb, grad_out, loss = pl.pallas_call(
        lambda *refs: plain_kernel(plain, coded, *refs),
        out_shape=(
            jax.ShapeDtypeStruct((2 * width, orbitals), F32),
            jax.ShapeDtypeStruct((width, width), F32),
            jax.ShapeDtypeStruct((1,), F32),
        ),
        in_specs=[pl.BlockSpec(memory_space=VM)],
        out_specs=(hbm, hbm, smem),
        scratch_shapes=[
            VM((2 * width, orbitals), F32),
            VM((width, width), F32),
            sem((count + 1,)),
        ],
        compiler_params=pltpu.CompilerParams(vmem_limit_bytes=VMEM_MIB * 1024 * 1024),
        name="decode",
    )(codes)
    return (grad_orb.reshape(2, width, orbitals), grad_out, loss)


def solution(mesh):
    in_specs = (
        P(None, ("parts", "walk"), "elec"),
        P(("parts", "elec"), None),
        P(("parts", "elec"), None),
        P(),
        P(("parts", "elec")),
        P("parts", None),
        P("parts", None),
        P("parts"),
        P(),
        P(),
        P(),
        P(),
        P(),
        P(("parts", "walk"), "elec", None),
    )
    out_specs = (P("parts", None, None), P("parts", None), P("parts"))
    return jax.shard_map(local, mesh=mesh, in_specs=in_specs, out_specs=out_specs, check_vma=False)
```

```python
import math

import jax
import jax.numpy as jnp
from jax import lax
from jax.experimental import pallas as pl
from jax.experimental.pallas import tpu as pltpu
from jax.sharding import PartitionSpec as P

HEADS = 16
BLOCK = 64
ATOM_DEV = 25
NEAR = 2
KMAX = 4
SLOT = 32
LANES = 128
WIDE = 256
TILE = 16
FULL = 32700.0
FINE = 64.0
HOP_US = 2.0
CORE_US = 1.0
CHUNK_US = 0.5
VMEM_MIB = 30
F32 = jnp.float32
BF16 = jnp.bfloat16
I16 = jnp.int16
VM = pltpu.VMEM
NT = (((1,), (1,)), ((), ()))


def encode(x):
    top = jnp.maximum(jnp.max(jnp.abs(x), axis=0, keepdims=True), 1e-30)
    level = jnp.ceil(jnp.log(top) * (FINE / math.log(2.0)))
    scale = jnp.exp2(level * (-1.0 / FINE)) * FULL
    return jnp.round(x * scale).astype(jnp.int32).astype(I16), level


def unit(level):
    return jnp.exp2(level * (1.0 / FINE)) * (1.0 / FULL)


def widen(codes):
    return codes.astype(jnp.int32).astype(F32)


def layout(piece, tail, blocks):
    plain, coded = [], []
    for c in range(blocks):
        plain.append((c * piece, piece, 0))
        coded.append((c * (piece + TILE), piece + TILE))
    plain.append((blocks * piece, 2 * tail, TILE))
    coded.append((blocks * (piece + TILE), 2 * tail + 2 * TILE))
    return plain, coded


def make_steps(pairs, walks, plain, coded, part, out, r1, s2, r2, a2, sz, r3, r4, *sems):
    send_core, recv_core, send_y, recv_y, send_z, recv_z, send_c, recv_c, send_b, recv_b = sems[:10]
    send_y2, recv_y2, send_core2, recv_core2 = sems[10:14]
    chunks = len(plain)
    elec = lax.axis_index("elec")
    wk = lax.axis_index("walk")
    core, y = lax.rem(elec, 2), elec // 2
    mesh_id = pl.DeviceIdType.MESH
    middle = walks // 2
    on_left = wk < middle
    level = jnp.where(on_left, wk, walks - 1 - wk)
    toward = jnp.where(on_left, 1, walks - 1)
    partner = {"elec": y * 2 + 1 - core}
    inward = {"walk": lax.rem(wk + toward, walks)}
    outward = {"walk": lax.rem(wk + walks - toward, walks)}
    inner_level = middle - 1

    def over_y(k):
        return {"elec": lax.rem(y + 1 + k, pairs) * 2 + core}

    def route(src, dst, ssem, rsem, peer):
        return pltpu.make_async_remote_copy(
            src_ref=src,
            dst_ref=dst,
            send_sem=ssem,
            recv_sem=rsem,
            device_id=peer,
            device_id_type=mesh_id,
        )

    def copies(c):
        low, size, extra = plain[c]
        rng = pl.ds(low, size + extra)
        code = pl.ds(*coded[c])
        whole = out.at[core, :, code]
        mine = out.at[core, y, code]
        return dict(
            core=route(
                part.at[1 - core, :, rng], r1.at[:, rng], send_core.at[c], recv_core.at[c], partner
            ),
            y=[
                route(s2.at[k, code], r2.at[k, code], send_y.at[c, k], recv_y.at[c, k], over_y(k))
                for k in range(pairs - 1)
            ],
            z=route(sz.at[code], r3.at[code], send_z.at[c], recv_z.at[c], inward),
            c=route(sz.at[code], r4.at[code], send_c.at[c], recv_c.at[c], inward),
            b=route(mine, mine, send_b.at[c], recv_b.at[c], outward),
            y2=[
                route(mine, mine, send_y2.at[c, k], recv_y2.at[c, k], over_y(k))
                for k in range(pairs - 1)
            ],
            core2=route(whole, whole, send_core2.at[c], recv_core2.at[c], partner),
        )

    flights = [copies(c) for c in range(chunks)]

    def spans(c):
        low, size, extra = plain[c]
        start = coded[c][0]
        groups = [(pl.ds(low, size), pl.ds(start, size))]
        if extra:
            groups.append((pl.ds(low + size, extra), pl.ds(start + size, extra)))
        return groups, pl.ds(start + size + extra, TILE)

    def code_into(c, read, dst):
        groups, scales = spans(c)
        row = lax.broadcasted_iota(jnp.int32, (TILE, LANES), 0)
        marks = None
        for g, (rows, codes) in enumerate(groups):
            body, mark = encode(read(rows))
            dst[codes] = body
            mark = jnp.broadcast_to(mark, (TILE, LANES))
            marks = mark if marks is None else jnp.where(row < TILE // 2, marks, mark)
        dst[scales] = marks.astype(jnp.int32).astype(I16)

    def decoded(c, src):
        groups, scales = spans(c)
        marks = widen(src[scales])
        return [
            (rows, widen(src[codes]) * unit(marks[g * (TILE // 2) : g * (TILE // 2) + 1]))
            for g, (rows, codes) in enumerate(groups)
        ]

    def send_inward(c, key):
        code_into(c, lambda rows: a2[rows], sz)
        flights[c][key].start()

    def pair_done(c):
        flight = flights[c]
        low, size, extra = plain[c]
        rng = pl.ds(low, size + extra)
        flight["core"].wait_recv()
        for k in range(pairs - 1):
            other = lax.rem(y + 1 + k, pairs)
            code_into(c, lambda rows: r1[other, rows] + part[core, other, rows], s2.at[k])
            flight["y"][k].start()
        a2[rng] = r1[y, rng] + part[core, y, rng]

    def step(stage, c):
        flight = flights[c]
        if stage == 0:
            for k, copy in enumerate(flight["y"]):
                copy.wait_recv()
                for rows, value in decoded(c, r2.at[k]):
                    a2[rows] = a2[rows] + value

            if inner_level > 0:

                @pl.when(level == 0)
                def _():
                    send_inward(c, "z")

        elif stage < middle:

            @pl.when(level == stage)
            def _():
                flight["z"].wait_recv()
                for rows, value in decoded(c, r3):
                    a2[rows] = a2[rows] + value
                if stage < inner_level:
                    send_inward(c, "z")

        if stage == inner_level:

            @pl.when(level == inner_level)
            def _():
                send_inward(c, "c")

        back = stage - middle
        if back == 0:

            @pl.when(level == inner_level)
            def _():
                own = decoded(c, sz)
                flight["c"].wait_recv()
                for (rows, value), (_, other) in zip(own, decoded(c, r4)):
                    a2[rows] = value + other
                code_into(c, lambda rows: a2[rows], out.at[core, y])
                if inner_level > 0:
                    flight["b"].start()
                for copy in flight["y2"]:
                    copy.start()
        elif 0 < back < middle:

            @pl.when(level == inner_level - back)
            def _():
                flight["b"].wait_recv()
                if back < inner_level:
                    flight["b"].start()
                for copy in flight["y2"]:
                    copy.start()

        if back == middle:
            for copy in flight["y2"]:
                copy.wait_recv()
            flight["core2"].start()
        elif back == middle + 1:
            flight["core2"].wait_recv()

    def begin(c):
        flights[c]["core"].start()

    stages = 2 * middle + 2

    def after(done):
        events = [(t, -1, c) for c, t in enumerate(done)]
        ready = list(done)
        for stage in range(stages):
            wait = CORE_US if stage == stages - 1 else HOP_US
            before = -1e9
            for c in range(chunks):
                before = max(ready[c] + wait, before + CHUNK_US)
                ready[c] = before
                events.append((before, stage, c))
        return sorted(events)

    def drain():
        for flight in flights:
            for copy in [flight["core"], flight["core2"]] + flight["y"] + flight["y2"]:
                copy.wait_send()

            @pl.when(level < inner_level)
            def _():
                flight["z"].wait_send()

            @pl.when(level == inner_level)
            def _():
                flight["c"].wait_send()

            @pl.when(level > 0)
            def _():
                flight["b"].wait_send()

    return begin, pair_done, step, after, drain


def thirds(x):
    rest = x - x.astype(BF16).astype(F32)
    return x, rest, rest - rest.astype(BF16).astype(F32)


def step_kernel(
    count,
    walks,
    near_ref,
    pairs_ref,
    pair_n_ref,
    emb,
    pos,
    epos,
    spin,
    *rest,
):
    outer, result, inner = rest[:7], rest[7], rest[8:-4]
    near, pairs, pair_n, table_sem = rest[-4:]
    gemb, gpos, gep, gsp = inner[:4]
    held = inner[4:11]
    spin_emb, w_query, w_key, w_value, w_out, w_orb, target = held
    send, recv, local_sem = inner[11:14]
    pstack, estack, e_s, q_s, v_s, kt_s, h_s, att_s, part = inner[14:23]
    me = lax.axis_index("elec")
    barrier = pltpu.get_barrier_semaphore()
    for k in range(count - 1):
        pl.semaphore_signal(
            barrier,
            inc=1,
            device_id={"elec": lax.rem(me + 1 + k, count)},
            device_id_type=pl.DeviceIdType.MESH,
        )
    wk = lax.axis_index("walk")

    @pl.when(wk > 0)
    def _():
        pl.semaphore_signal(
            barrier,
            inc=1,
            device_id={"walk": lax.rem(wk + walks - 1, walks)},
            device_id_type=pl.DeviceIdType.MESH,
        )

    @pl.when(wk < walks - 1)
    def _():
        pl.semaphore_signal(
            barrier,
            inc=1,
            device_id={"walk": lax.rem(wk + 1, walks)},
            device_id_type=pl.DeviceIdType.MESH,
        )

    ends = jnp.where(wk > 0, 1, 0) + jnp.where(wk < walks - 1, 1, 0)
    small = ((emb, gemb), (pos, gpos), (epos, gep), (spin, gsp))
    own = [
        pltpu.make_async_copy(src, dst.at[me], local_sem.at[i])
        for i, (src, dst) in enumerate(small)
    ]
    loads = [
        pltpu.make_async_copy(src, dst, local_sem.at[4 + i])
        for i, (src, dst) in enumerate(zip(outer, held))
    ]
    tables = [
        pltpu.make_async_copy(src, dst, table_sem.at[i])
        for i, (src, dst) in enumerate(
            ((near_ref, near), (pairs_ref, pairs), (pair_n_ref, pair_n))
        )
    ]
    for copy in own + tables + loads:
        copy.start()
    for copy in own:
        copy.wait()
    pl.semaphore_wait(barrier, count - 1 + ends)
    copies = []
    turns = count // 2
    chip, side = me // 2, lax.rem(me, 2)
    for k in range(count - 1):
        far = lax.rem(chip + 1 + k // 2, turns) * 2 + (side if k % 2 == 0 else 1 - side)
        peer = far if k < count - 2 else chip * 2 + 1 - side
        for i, (_, dst) in enumerate(small):
            copy = pltpu.make_async_remote_copy(
                src_ref=dst.at[me],
                dst_ref=dst.at[me],
                send_sem=send.at[k, i],
                recv_sem=recv.at[k, i],
                device_id={"elec": peer},
                device_id_type=pl.DeviceIdType.MESH,
            )
            copy.start()
            copies.append(copy)
    walkers, rows = gep.shape[2], gep.shape[3]
    width = w_query.shape[0]
    head = width // HEADS
    per_device = rows // BLOCK
    owners = (me, lax.rem(me + count - 1, count), lax.rem(me + 1, count))
    pstack[...] = jnp.zeros_like(pstack)
    estack[...] = jnp.zeros_like(estack)
    e_s[...] = jnp.zeros_like(e_s)
    first_half = lax.broadcasted_iota(jnp.int32, (width, 2 * BLOCK), 1) < BLOCK
    depth = NEAR * SLOT
    lane_id = lax.broadcasted_iota(jnp.int32, (BLOCK, 2 * depth), 1)
    low_lanes = lax.broadcasted_iota(jnp.int32, (walkers * BLOCK, 2 * depth), 1) < depth
    for copy in tables:
        copy.wait()
    places, valid = [], []
    for p in range(per_device):
        query_block = me * per_device + p
        for slot in range(KMAX):
            used = slot < pair_n[0, query_block]
            key_block = jnp.where(used, pairs[slot, query_block], query_block)
            away = lax.rem(key_block // per_device - me + count, count)
            side = jnp.where(away == 0, 0, jnp.where(away == 1, 2, 1))
            places.append(side * per_device + lax.rem(key_block, per_device))
            valid.append(jnp.where(used, 1.0, 0.0).astype(F32))
    for copy in loads[:4]:
        copy.wait()
    wk_t = w_key[...].astype(F32).T.astype(BF16)
    for copy in copies:
        copy.wait_recv()
    spin_cols = []
    for j, owner in enumerate(owners):
        for p in range(per_device):
            for n in range(NEAR):
                group = near[n, owner * per_device + p]
                for low in (n * SLOT, depth + n * SLOT):
                    pstack[j, p, 0:3, low : low + ATOM_DEV] = gpos[group]
                estack[j, p, n * SLOT : n * SLOT + ATOM_DEV, :] = gemb[group]
            estack[j, p, ATOM_DEV : ATOM_DEV + 2, :] = spin_emb[...]
        electron = gep[owner]
        for axis in range(3):
            e_s[j, axis * walkers : (axis + 1) * walkers, :] = electron[axis]
        e_s[j, 3 * walkers : 3 * walkers + 1, :] = gsp[owner].astype(F32)
        columns = e_s[j].T
        up_one = columns[:, 3 * walkers : 3 * walkers + 1]
        spin_cols.append(up_one)
        blocks = []
        for p in range(per_device):
            pieces = []
            mine = slice(p * BLOCK, (p + 1) * BLOCK)
            up = up_one[mine]
            for w in range(walkers):
                distance = jnp.zeros((BLOCK, 2 * depth), F32)
                for axis in range(3):
                    at = axis * walkers + w
                    spacing = columns[mine, at : at + 1] - pstack[j, p, axis : axis + 1, :]
                    distance = distance + spacing * spacing
                close = 1.0 / (1.0 + distance)
                close = jnp.where(lane_id % depth == ATOM_DEV, 1.0 - up, close)
                close = jnp.where(lane_id % depth == ATOM_DEV + 1, up, close)
                pieces.append(close)
            one, two, three = thirds(jnp.concatenate(pieces, axis=0))
            high = jnp.where(low_lanes, one, two).astype(BF16)
            rest = jnp.where(low_lanes, one, three).astype(BF16)
            e_one, e_two, e_three = [part.astype(BF16) for part in thirds(estack[j, p])]
            blocks.append(
                jnp.dot(
                    jnp.concatenate([high, high, rest], axis=1),
                    jnp.concatenate([e_one, e_one, e_two, e_two, e_three, e_one], axis=0),
                    preferred_element_type=F32,
                ).astype(BF16)
            )
        hidden = jnp.concatenate(blocks, axis=0)
        values = jnp.dot(hidden, w_value[...], preferred_element_type=F32).astype(BF16)
        keys_t = lax.dot_general(wk_t, hidden, NT, preferred_element_type=F32)
        for p in range(per_device):
            at = j * per_device + p
            for w in range(walkers):
                start = (p * walkers + w) * BLOCK
                v_s[w, at] = values[start : start + BLOCK]
            for w in range(0, walkers, 2):
                start = (p * walkers + w) * BLOCK
                across = keys_t[:, start : start + 2 * BLOCK]
                turned = jnp.concatenate([across[:, BLOCK:], across[:, :BLOCK]], axis=1)
                kt_s[w, at] = jnp.where(first_half, across, turned).astype(BF16)
                kt_s[w + 1, at] = jnp.where(first_half, turned, across).astype(BF16)
        if j == 0:
            queries = jnp.dot(hidden, w_query[...], preferred_element_type=F32).astype(BF16)
            queries = (queries.astype(F32) * (1.0 / math.sqrt(head))).astype(BF16)
            for w in range(walkers):
                for p in range(per_device):
                    start = (p * walkers + w) * BLOCK
                    h_s[w, p] = hidden[start : start + BLOCK]
                    q_s[w, p] = queries[start : start + BLOCK]
    group = rows // head
    head_lane = lax.broadcasted_iota(jnp.int32, (BLOCK, rows), 1) // head
    head_masks = [jnp.where(head_lane == h, 1.0, 0.0).astype(BF16) for h in range(group)]
    half_row = lax.broadcasted_iota(jnp.int32, (1, 2 * BLOCK), 1) < BLOCK

    def listed(w, p):
        slots = range(p * KMAX, (p + 1) * KMAX)
        values = jnp.concatenate([v_s[w, places[s]] for s in slots], axis=0)
        keys_t = jnp.concatenate(
            [
                jnp.where(first_half, kt_s[w, places[s]], kt_s[w, places[s + 1]])
                for s in slots[::2]
            ],
            axis=1,
        )
        allowed = jnp.concatenate(
            [jnp.where(half_row, valid[s], valid[s + 1]) for s in slots[::2]], axis=1
        )
        return values, keys_t, allowed

    def score(w, p, low, keys_t):
        query = q_s[w, p, :, low : low + rows]
        spread = jnp.concatenate([query * mask for mask in head_masks], axis=0)
        return jnp.dot(spread, keys_t[low : low + rows], preferred_element_type=F32)

    def attend(w, p, low, scores, values, allowed):
        top = jnp.max(scores, axis=1, keepdims=True)
        weights = jnp.exp(scores - top) * allowed
        total = jnp.sum(weights, axis=1, keepdims=True)
        mixed = jnp.dot(
            weights.astype(BF16), values[:, low : low + rows], preferred_element_type=F32
        )
        above, below = mixed[:BLOCK], jnp.broadcast_to(total[:BLOCK], (BLOCK, rows))
        for h in range(1, group):
            mine = slice(h * BLOCK, (h + 1) * BLOCK)
            above = jnp.where(head_lane == h, mixed[mine], above)
            below = jnp.where(head_lane == h, total[mine], below)
        att_s[w, p * BLOCK : (p + 1) * BLOCK, low : low + rows] = above / below

    waiting = None
    for w in range(walkers):
        for p in range(per_device):
            values, keys_t, allowed = listed(w, p)
            for low in range(0, width, rows):
                scores = score(w, p, low, keys_t)
                if waiting is not None:
                    attend(*waiting)
                waiting = (w, p, low, scores, values, allowed)
    attend(*waiting)
    for copy in loads[4:]:
        copy.wait()
    attended_wide = jnp.concatenate([att_s[w] for w in range(walkers)], axis=0)
    attended = attended_wide.astype(BF16)
    mixed_out = jnp.dot(attended, w_out[...], preferred_element_type=F32)
    hidden = h_s[...].reshape(walkers * rows, width).astype(F32)
    hidden_out = (hidden + mixed_out).astype(BF16).astype(F32)
    spin_row = gsp[me].astype(F32)
    spin_col = spin_cols[0]
    up_col = jnp.concatenate([spin_col] * walkers, axis=0) > 0.5
    up_lane = jnp.concatenate([spin_row] * walkers, axis=1) > 0.5
    split = jnp.concatenate(
        [jnp.where(up_col, 0.0, hidden_out), jnp.where(up_col, hidden_out, 0.0)], axis=1
    ).astype(BF16)
    hidden_t = hidden_out.T
    split_t = jnp.concatenate(
        [jnp.where(up_lane, 0.0, hidden_t), jnp.where(up_lane, hidden_t, 0.0)], axis=0
    ).astype(BF16)
    orbitals = target.shape[1]
    both_rows = 2 * width
    pairs = count // 2
    piece = both_rows // count
    tail = width // count
    blocks = orbitals // LANES
    plain, coded = layout(piece, tail, blocks)
    begin, pair_done, step, after, drain = make_steps(
        pairs, walks, plain, coded, part, result, *inner[23:]
    )
    share = 1.0 / (walkers * rows * count * lax.axis_size("walk"))
    backward = None
    loss = jnp.zeros((1, WIDE), F32)
    halves = WIDE // LANES
    for c in range(orbitals // WIDE):
        columns = slice(c * WIDE, (c + 1) * WIDE)
        w_piece = w_orb[:, columns]
        residual = jnp.dot(split, w_piece, preferred_element_type=F32) - target[
            :, columns
        ].astype(F32)
        loss = loss + jnp.sum(residual * residual, axis=0, keepdims=True)
        signal = residual.astype(BF16)
        grad = share * jnp.dot(split_t, signal, preferred_element_type=F32)
        for h in range(halves):
            low = plain[halves * c + h][0]
            for q in range(count):
                part[q // pairs, q % pairs, low : low + piece, :] = grad[
                    q * piece : (q + 1) * piece, h * LANES : (h + 1) * LANES
                ]
            begin(halves * c + h)
        if c > 0:
            for h in range(halves):
                pair_done(halves * (c - 1) + h)
        term = lax.dot_general(signal, w_piece, NT, preferred_element_type=F32)
        backward = term if backward is None else backward + term
    chosen = jnp.where(up_col, backward[:, width:], backward[:, :width]).astype(BF16)
    att_t = attended_wide.T.astype(BF16)
    grad = share * jnp.dot(att_t, chosen, preferred_element_type=F32)
    spread = (0.5 * share) * jnp.sum(loss, axis=1, keepdims=True)
    base = plain[-1][0]
    for q in range(count):
        here = part.at[q // pairs, q % pairs]
        for h in range(halves):
            here[base + h * tail : base + (h + 1) * tail, :] = grad[
                q * tail : (q + 1) * tail, h * LANES : (h + 1) * LANES
            ]
        here[base + halves * tail : base + halves * tail + TILE, :] = jnp.broadcast_to(
            spread, (TILE, LANES)
        )
    begin(blocks)
    early = blocks - halves
    done = [(c // halves) * 0.7 - 2.0 if c < early else 0.3 * (c - early) for c in range(blocks + 1)]
    for _, stage, c in after(done):
        if stage >= 0:
            step(stage, c)
        elif c >= early:
            pair_done(c)
    drain()
    for copy in copies:
        copy.wait_send()


def plain_kernel(plain, coded, codes, g_orb, g_out, g_loss, orb, low, sems):
    pairs = codes.shape[1]
    count = 2 * pairs
    piece, tail = orb.shape[0] // count, low.shape[0] // count
    copies = []
    def emit(src, dst):
        copy = pltpu.make_async_copy(src, dst, sems.at[len(copies)])
        copy.start()
        copies.append(copy)

    for q in range(count):
        here = codes.at[q // pairs, q % pairs]
        rows = slice(q * piece, (q + 1) * piece)
        for c, ((_, size, extra), (start, length)) in enumerate(zip(plain, coded)):
            marks = widen(here[start + size + extra : start + length])
            value = widen(here[start : start + size]) * unit(marks[:1])
            if not extra:
                orb[rows, c * LANES : (c + 1) * LANES] = value
                continue
            for h in range(low.shape[1] // LANES):
                low[q * tail : (q + 1) * tail, h * LANES : (h + 1) * LANES] = value[
                    h * tail : (h + 1) * tail
                ]
        emit(orb.at[rows], g_orb.at[rows])
        if q == 0:
            mark = marks[TILE // 2 : TILE // 2 + 1]
            sums = widen(here[start + size : start + size + extra]) * unit(mark)
            g_loss[0] = jnp.max(sums)
    emit(low, g_out)
    for copy in copies:
        copy.wait()


def pinned(*arrays):
    return [pltpu.with_memory_space_constraint(array, pltpu.HBM) for array in arrays]


def local(
    elec_pos,
    atom_pos,
    atom_emb,
    spin_emb,
    spin,
    near_atoms,
    pair_list,
    pair_count,
    w_query,
    w_key,
    w_value,
    w_out,
    w_orb,
    target,
):
    walkers, rows = elec_pos.shape[1], elec_pos.shape[2]
    count, walks = lax.axis_size("elec"), lax.axis_size("walk")
    width, orbitals = w_query.shape[0], w_orb.shape[2]
    row_local = walkers * rows
    smem = pl.BlockSpec(memory_space=pltpu.SMEM)
    sem = pltpu.SemaphoreType.DMA
    hbm = pl.BlockSpec(memory_space=pltpu.HBM)
    pairs = count // 2
    plain, coded = layout(2 * width // count, width // count, orbitals // LANES)
    chunks = len(plain)
    height = sum(plain[-1])
    long = sum(coded[-1])
    one, many = sem((chunks,)), sem((chunks, pairs - 1))
    depth = NEAR * SLOT
    lists = (near_atoms.T, pair_list.T, pair_count.reshape(1, -1))
    codes = pl.pallas_call(
        lambda *refs: step_kernel(count, walks, *refs),
        out_shape=VM((2, pairs, long, LANES), I16),
        in_specs=[hbm] * 14,
        out_specs=pl.BlockSpec(memory_space=VM),
        scratch_shapes=[
            VM((count, ATOM_DEV, width), F32),
            VM((count, 3, ATOM_DEV), F32),
            VM((count, 3, walkers, rows), F32),
            VM((count, 1, rows), jnp.int32),
            VM((2, width), F32),
            VM((width, width), BF16),
            VM((width, width), BF16),
            VM((width, width), BF16),
            VM((width, width), BF16),
            VM((2 * width, orbitals), BF16),
            VM((row_local, orbitals), BF16),
            sem((count - 1, 4)),
            sem((count - 1, 4)),
            sem((11,)),
            VM((3, rows // BLOCK, 8, 2 * depth), F32),
            VM((3, rows // BLOCK, depth, width), F32),
            VM((3, rows, rows), F32),
            VM((walkers, rows // BLOCK, BLOCK, width), BF16),
            VM((walkers, 3 * rows // BLOCK, BLOCK, width), BF16),
            VM((walkers, 3 * rows // BLOCK, width, 2 * BLOCK), BF16),
            VM((walkers, rows // BLOCK, BLOCK, width), BF16),
            VM((walkers, rows, width), F32),
            VM((2, pairs, height, LANES), F32),
            VM((pairs, height, LANES), F32),
            VM((pairs - 1, long, LANES), I16),
            VM((pairs - 1, long, LANES), I16),
            VM((height, LANES), F32),
            VM((long, LANES), I16),
            VM((long, LANES), I16),
            VM((long, LANES), I16),
        ]
        + [one] * 2
        + [many] * 2
        + [one] * 6
        + [many] * 2
        + [one] * 2
        + [pltpu.SMEM(table.shape, jnp.int32) for table in lists]
        + [sem((3,))],
        compiler_params=pltpu.CompilerParams(
            collective_id=0, has_side_effects=True, vmem_limit_bytes=VMEM_MIB * 1024 * 1024
        ),
        name="whole_step",
    )(
        *pinned(
        *lists,
        atom_emb,
        atom_pos.T,
        elec_pos,
        spin.reshape(1, rows),
        spin_emb,
        w_query,
        w_key,
        w_value,
        w_out,
        w_orb.reshape(2 * width, orbitals),
        target.reshape(row_local, orbitals),
        )
    )
    piece, tail = 2 * width // count, width // count
    grad_orb, grad_out, loss = pl.pallas_call(
        lambda *refs: plain_kernel(plain, coded, *refs),
        out_shape=(
            jax.ShapeDtypeStruct((2 * width, orbitals), F32),
            jax.ShapeDtypeStruct((width, width), F32),
            jax.ShapeDtypeStruct((1,), F32),
        ),
        in_specs=[pl.BlockSpec(memory_space=VM)],
        out_specs=(hbm, hbm, smem),
        scratch_shapes=[
            VM((2 * width, orbitals), F32),
            VM((width, width), F32),
            sem((count + 1,)),
        ],
        compiler_params=pltpu.CompilerParams(vmem_limit_bytes=VMEM_MIB * 1024 * 1024),
        name="decode",
    )(codes)
    return (grad_orb.reshape(2, width, orbitals), grad_out, loss)


def solution(mesh):
    in_specs = (
        P(None, ("parts", "walk"), "elec"),
        P(("parts", "elec"), None),
        P(("parts", "elec"), None),
        P(),
        P(("parts", "elec")),
        P("parts", None),
        P("parts", None),
        P("parts"),
        P(),
        P(),
        P(),
        P(),
        P(),
        P(("parts", "walk"), "elec", None),
    )
    out_specs = (P("parts", None, None), P("parts", None), P("parts"))
    return jax.shard_map(local, mesh=mesh, in_specs=in_specs, out_specs=out_specs, check_vma=False)
```
